128 devices in a mesh: ctx: 16 (over y, z_hi, core), head: 8 (over x, z_lo).
Axes of the slice: x: 4, y: 4, z: 4 (z_hi: 2, z_lo: 2; z = z_hi * 2 + z_lo), core: 2. Of those that a mesh axis runs over, the one named last changes fastest.
Arguments:
- queries: bfloat16 [2048, 12288], P('ctx', 'head'), may hold values from -8 to 8
- latents: bfloat16 [2048, 512], P('ctx'), may hold values from -4 to 4
- rope_key: bfloat16 [2048, 64], P('ctx'), may hold values from -8 to 8
- up_key_weight: bfloat16 [512, 8192], P(None, 'head'), may hold values from -0.5 to 0.5
- up_value_weight: bfloat16 [512, 8192], P(None, 'head'), may hold values from -0.25 to 0.25
- out_grad: bfloat16 [2048, 8192], P('ctx', 'head'), may hold values from -6 to 6
- group_order: int32 [32], replicated, may hold values from 0 to 31, as said below
Outputs:
- query_grad: bfloat16 [2048, 12288], P('ctx', 'head')
- latent_grad: float32 [2048, 512], P('ctx')
- rope_grad: float32 [2048, 64], P('ctx')
- up_key_grad: float32 [512, 8192], P('ctx', 'head')
- up_value_grad: float32 [512, 8192], P('ctx', 'head')
The draws below stay inside these ranges and needn't reach their ends.
Inputs may be any that keep to these rules, and one draw needn't show every extreme that they name: A permutation of the 32 group numbers; storage slot k (rows k * 64 to k * 64 + 63) holds the sequence positions group_order[k] * 64 on, in order.
All inputs are finite; a program needn't handle non-finite values.
Results may differ from the reference program's by a relative error of at most 0.017.
Values may be sent and summed in bfloat16 or wider, within the bound.
No kernel may reach another device: no remote copies, remote signals or barrier semaphores. Data moves between devices by JAX's collectives and lax.ppermute only.
A program may use at most 64 MiB of HBM per device.

```python
import jax
import jax.numpy as jnp
from jax import lax

D_LATENT = 512
ROPE = 64
NOPE = 128
VDIM = 128
HEADS = 64
TOKENS = 2048
GROUP = 64
GROUPS = 32


def draw_rope_key(key, part):
    values = jax.random.normal(jax.random.fold_in(key, 5), (TOKENS, ROPE), jnp.float32)
    return jnp.clip(values, -8.0, 8.0).astype(jnp.bfloat16)


def draw_queries(key, part):
    values = jax.random.normal(jax.random.fold_in(key, 9), (TOKENS, HEADS * (NOPE + ROPE)), jnp.float32)
    return jnp.clip(values, -8.0, 8.0).astype(jnp.bfloat16)


def draw_group_order(key, part):
    return jax.random.permutation(jax.random.fold_in(key, 3), GROUPS).astype(jnp.int32)


def shard_levels(stream_key, shape, shards, low, largest):
    factor_of, own = 1.0, jax.random.fold_in(stream_key, 6)
    for dim, parts in shards:
        heights = jnp.exp(jax.random.uniform(jax.random.fold_in(own, dim), (parts,), jnp.float32, low / len(shards), largest / len(shards)))
        factor_of = factor_of * jnp.repeat(heights, shape[dim] // parts).reshape([-1 if axis == dim else 1 for axis in range(len(shape))])
    return factor_of


def normal_values(stream_key, shape, scale, bound, pieces=(), kind=jnp.bfloat16):
    drawn = jax.random.normal(stream_key, shape, jnp.float32) * scale
    if len(pieces) > 0:
        drawn = shard_levels(stream_key, shape, pieces, -0.22, 0.18) * drawn
    return jnp.clip(drawn, min=-bound, max=bound).astype(kind)


def setup_inputs(seed: int = 0) -> dict:
    seeds = jax.random.split(jax.random.key(seed), 8)
    return {
        "queries": draw_queries(jax.random.fold_in(seeds[7], 71), 0),
        "latents": normal_values(seeds[1], (TOKENS, D_LATENT), 0.5, 4.0, ((0, 16),)),
        "rope_key": draw_rope_key(jax.random.fold_in(seeds[7], 71), 0),
        "up_key_weight": normal_values(seeds[3], (D_LATENT, HEADS * NOPE), NOPE ** -0.5, 0.5, ((1, 8),)),
        "up_value_weight": normal_values(seeds[4], (D_LATENT, HEADS * VDIM), D_LATENT ** -0.5, 0.25, ((1, 8),)),
        "out_grad": normal_values(seeds[5], (TOKENS, HEADS * VDIM), 1.0, 6.0, ((0, 16), (1, 8))),
        "group_order": draw_group_order(jax.random.fold_in(seeds[7], 71), 0),
    }


NEG_FILL = -1.0e30


def reference(queries, latents, rope_key, up_key_weight, up_value_weight, out_grad, group_order):
    scale_factor = (NOPE + ROPE) ** -0.5
    head_width = NOPE + ROPE
    row_ids = jnp.arange(TOKENS, dtype=jnp.int32)
    positions = group_order[row_ids // GROUP] * GROUP + row_ids % GROUP
    visible = positions[None, :] <= positions[:, None]

    def one_head(carried, head_index):
        all_latent, all_rope = carried
        query_head = lax.dynamic_slice_in_dim(queries, head_index * head_width, head_width, 1)
        query_nope = query_head[:, :NOPE]
        query_rope = query_head[:, NOPE:]
        up_key = lax.dynamic_slice_in_dim(up_key_weight, head_index * NOPE, NOPE, 1)
        up_value = lax.dynamic_slice_in_dim(up_value_weight, head_index * VDIM, VDIM, 1)
        grad_head = lax.dynamic_slice_in_dim(out_grad, head_index * VDIM, VDIM, 1)
        query_abs = jnp.dot(query_nope, up_key.T, preferred_element_type=jnp.float32).astype(jnp.bfloat16)
        grad_lat = jnp.dot(grad_head, up_value.T, preferred_element_type=jnp.float32).astype(jnp.bfloat16)
        scores = (jnp.dot(query_abs, latents.T, preferred_element_type=jnp.float32)
                  + jnp.dot(query_rope, rope_key.T, preferred_element_type=jnp.float32)) * scale_factor
        row_max = jnp.max(jnp.where(visible, scores, NEG_FILL), axis=1, keepdims=True)
        log_total = row_max + jnp.log(jnp.sum(jnp.where(visible, jnp.exp(scores - row_max), 0.0), axis=1, keepdims=True))
        softmax_rows = jnp.where(visible, jnp.exp(scores - log_total), 0.0)
        grad_prob = jnp.dot(grad_lat, latents.T, preferred_element_type=jnp.float32)
        row_delta = jnp.sum(softmax_rows * grad_prob, axis=1, keepdims=True)
        grad_score = softmax_rows * (grad_prob - row_delta) * scale_factor
        probs_low = softmax_rows.astype(jnp.bfloat16)
        grad_low = grad_score.astype(jnp.bfloat16)
        out_latent = jnp.dot(probs_low, latents, preferred_element_type=jnp.float32).astype(jnp.bfloat16)
        grad_abs = jnp.dot(grad_low, latents, preferred_element_type=jnp.float32).astype(jnp.bfloat16)
        grad_nope = jnp.dot(grad_abs, up_key, preferred_element_type=jnp.float32)
        grad_rope = jnp.dot(grad_low, rope_key, preferred_element_type=jnp.float32)
        query_part = jnp.concatenate([grad_nope, grad_rope], axis=1).astype(jnp.bfloat16)
        latent_part = (jnp.dot(grad_low.T, query_abs, preferred_element_type=jnp.float32)
                       + jnp.dot(probs_low.T, grad_lat, preferred_element_type=jnp.float32))
        rope_part = jnp.dot(grad_low.T, query_rope, preferred_element_type=jnp.float32)
        key_part = jnp.dot(grad_abs.T, query_nope, preferred_element_type=jnp.float32)
        value_part = jnp.dot(out_latent.T, grad_head, preferred_element_type=jnp.float32)
        return (all_latent + latent_part, all_rope + rope_part), (query_part, key_part, value_part)

    initial = (jnp.zeros((TOKENS, D_LATENT), jnp.float32), jnp.zeros((TOKENS, ROPE), jnp.float32))
    sums, stacked = lax.scan(one_head, initial, jnp.arange(HEADS, dtype=jnp.int32))
    latent_grad, rope_grad = sums
    query_parts, key_parts, value_parts = stacked
    query_grad = jnp.transpose(query_parts, (1, 0, 2)).reshape(TOKENS, HEADS * head_width)
    up_key_grad = jnp.transpose(key_parts, (1, 0, 2)).reshape(D_LATENT, HEADS * NOPE)
    up_value_grad = jnp.transpose(value_parts, (1, 0, 2)).reshape(D_LATENT, HEADS * VDIM)
    return query_grad, latent_grad, rope_grad, up_key_grad, up_value_grad
```

```python
import functools
import math

import jax
import jax.numpy as jnp
from jax import lax
from jax.experimental import pallas as pl
from jax.experimental.pallas import tpu as pltpu
from jax.sharding import PartitionSpec as P

D_LATENT = 512
ROPE = 64
NOPE = 128
VDIM = 128
WIDTH = D_LATENT + ROPE
GROUP = 64
NEG_FILL = -1e30
SCALE = (NOPE + ROPE) ** -0.5
SCALE_LOG2 = SCALE * math.log2(math.e)

CTX = 16
HEAD = 8
BF16 = jnp.bfloat16
F32 = jnp.float32


def ctx_xor(position):
    core, y_bits, zhi = position >> 3, (position >> 1) & 3, position & 1
    return (y_bits << 2) | (zhi << 1) | core


def swap_ctx(value, mask):
    return lax.ppermute(value, "ctx", [(i, i ^ mask) for i in range(CTX)])


def swap_head(value, mask):
    return lax.ppermute(value, "head", [(i, i ^ mask) for i in range(HEAD)])


def dot(a, b, dims):
    return lax.dot_general(a, b, (dims, ((), ())), preferred_element_type=F32)


NT = ((1,), (1,))
NN = ((1,), (0,))
TN = ((0,), (0,))

BLOCK = 256
BLOCKS = 8
PAIRS = 4


def scores_kernel(*refs):
    k_refs = refs[:BLOCKS]
    q_ref, gl_ref, bias_ref = refs[BLOCKS : BLOCKS + 3]
    probs_out, grads_out, send_ref = refs[BLOCKS + 3 : BLOCKS + 6]
    probs, grads, e_ref, g_ref, sems = refs[BLOCKS + 6 :]
    step = pl.program_id(0)

    @pl.when(step < PAIRS)
    def _():
        q = q_ref[step]
        gl = gl_ref[step]
        run_max, run_sum, run_dot = None, None, None
        maxes = []
        for kb in range(BLOCKS):
            rows = slice(kb * BLOCK, (kb + 1) * BLOCK)
            keys = k_refs[kb][...]
            s = dot(keys, q, NT)
            g = dot(keys[:, :D_LATENT], gl, NT)
            bias = bias_ref[rows, :]
            s = s * SCALE_LOG2 + jnp.concatenate([bias, bias], axis=1)
            top = jnp.max(s, axis=0, keepdims=True)
            if kb > 0:
                top = jnp.maximum(run_max, top)
            e = jnp.exp2(s - top)
            part = jnp.sum(e, axis=0, keepdims=True)
            part_dot = jnp.sum(e * g, axis=0, keepdims=True)
            if kb > 0:
                shrink = jnp.exp2(run_max - top)
                part = run_sum * shrink + part
                part_dot = run_dot * shrink + part_dot
            run_max, run_sum, run_dot = top, part, part_dot
            maxes.append(top)
            e_ref[rows, :] = e
            g_ref[rows, :] = g
        inverse = 1.0 / run_sum
        delta = run_dot * inverse
        for kb in range(BLOCKS):
            rows = slice(kb * BLOCK, (kb + 1) * BLOCK)
            factor = jnp.exp2(maxes[kb] - run_max) * inverse
            p = e_ref[rows, :] * factor
            probs[step, rows, :] = p.astype(BF16)
            grads[step, rows, :] = (p * (g_ref[rows, :] - delta) * SCALE).astype(BF16)
        pltpu.make_async_copy(probs.at[step], probs_out.at[step], sems.at[0, step]).start()
        pltpu.make_async_copy(grads.at[step], grads_out.at[step], sems.at[1, step]).start()

    @pl.when(step >= PAIRS)
    def _():
        base = (BLOCKS // 2) * BLOCK
        rows = pl.ds(pl.multiple_of(base + (step - PAIRS) * BLOCK, BLOCK), BLOCK)
        acc = latent_rows([probs[i, rows, :] for i in range(PAIRS)], [grads[i, rows, :] for i in range(PAIRS)], q_ref, gl_ref)
        send_ref[:, :D_LATENT] = acc[0].astype(BF16)
        send_ref[:, D_LATENT:] = acc[1].astype(BF16)

    @pl.when(step == pl.num_programs(0) - 1)
    def _():
        for i in range(PAIRS):
            pltpu.make_async_copy(probs.at[i], probs_out.at[i], sems.at[0, i]).wait()
            pltpu.make_async_copy(grads.at[i], grads_out.at[i], sems.at[1, i]).wait()


def latent_rows(probs, grads, q_ref, gl_ref):
    both, nope = None, None
    for i in range(PAIRS):
        a = dot(grads[i], q_ref[i], NN)
        b = dot(probs[i], gl_ref[i], NN)
        both = a if both is None else both + a
        nope = b if nope is None else nope + b
    return both[:, :D_LATENT] + nope, both[:, D_LATENT:]


def keep_kernel(probs_ref, grads_ref, q_ref, gl_ref, keep_ref):
    acc = latent_rows([probs_ref[i] for i in range(PAIRS)], [grads_ref[i] for i in range(PAIRS)], q_ref, gl_ref)
    keep_ref[:, :D_LATENT] = acc[0].astype(BF16)
    keep_ref[:, D_LATENT:] = acc[1].astype(BF16)


def weights_kernel(*refs):
    own_ref = refs[0]
    k_refs = refs[1 : BLOCKS + 1]
    probs_ref, grads_ref, query_ref, out_grad_ref, up_key_ref = refs[BLOCKS + 1 : BLOCKS + 6]
    query_grad_ref, send_ref, keep_ref = refs[BLOCKS + 6 : BLOCKS + 9]
    kt_ref, w_ref = refs[BLOCKS + 9 :]

    @pl.when(pl.program_id(0) == 0)
    def _():
        for kb in range(BLOCKS):
            kt_ref[:, kb * BLOCK : (kb + 1) * BLOCK] = k_refs[kb][...].T

    out_t = dot(kt_ref[:D_LATENT, :], probs_ref[...], NN).astype(BF16)
    abs_t = dot(kt_ref[...], grads_ref[...], NN)
    rope_t = abs_t[D_LATENT:, :]
    abs_t = abs_t[:D_LATENT, :].astype(BF16)
    queries = query_ref[...]
    pieces = []
    for h in range(2):
        cols = slice(h * NOPE, (h + 1) * NOPE)
        first = h * (NOPE + ROPE)
        nope = queries[:, first : first + NOPE]
        w_ref[0, :, cols] = dot(abs_t[:, cols], nope, NN).astype(BF16)
        w_ref[1, :, cols] = dot(out_t[:, cols], out_grad_ref[:, cols], NN).astype(BF16)
        pieces.append(dot(abs_t[:, cols], up_key_ref[:, cols], TN))
        pieces.append(rope_t[:, cols].T)
    query_grad_ref[...] = jnp.concatenate(pieces, axis=1).astype(BF16)
    own = own_ref[0]
    share = D_LATENT // CTX
    for position in range(CTX):
        rows = pl.ds(pl.multiple_of((own ^ ctx_xor(position)) * share, share), share)
        out = send_ref if position >= CTX // 2 else keep_ref
        out[position % (CTX // 2), 0] = w_ref[0, rows, :]
        out[position % (CTX // 2), 1] = w_ref[1, rows, :]


def spread_sum(parts):
    total = parts[0].astype(F32)
    for part in parts[1:]:
        total = total + part.astype(F32)
    return total


def per_device(queries, latents, rope_key, up_key_weight, up_value_weight, out_grad, group_order):
    tok = queries.shape[0]
    heads = up_key_weight.shape[1] // NOPE
    own = lax.axis_index("ctx").astype(jnp.int32)

    keys = jnp.concatenate([latents, rope_key], axis=1)
    keys = jnp.concatenate([keys, swap_ctx(keys, 2)], axis=0)
    near = [keys] + [swap_ctx(keys, k << 2) for k in (1, 2, 3)]
    far = [swap_ctx(k, 1) for k in near]
    k_blocks = near + far

    shaped = queries.reshape(tok, heads, NOPE + ROPE)
    up_key = up_key_weight.reshape(D_LATENT, heads, NOPE)
    up_value = up_value_weight.reshape(D_LATENT, heads, VDIM)
    grad_out = out_grad.reshape(tok, heads, VDIM)
    query_abs = jnp.einsum("thd,khd->htk", shaped[:, :, :NOPE], up_key, preferred_element_type=F32).astype(BF16)
    grad_lat = jnp.einsum("thd,khd->htk", grad_out, up_value, preferred_element_type=F32).astype(BF16)
    query_all = jnp.concatenate([query_abs, jnp.swapaxes(shaped[:, :, NOPE:], 0, 1)], axis=2)
    query_all = query_all.reshape(PAIRS, 2 * tok, WIDTH)
    grad_lat = grad_lat.reshape(PAIRS, 2 * tok, D_LATENT)

    xors = jnp.array([ctx_xor(p) for p in range(CTX)], jnp.int32)
    slots = ((own ^ xors)[:, None] * 2 + jnp.arange(2, dtype=jnp.int32)[None, :]).reshape(-1)
    table = jnp.arange(group_order.shape[0], dtype=jnp.int32)
    groups = jnp.sum(jnp.where(slots[:, None] == table[None, :], group_order[None, :], 0), axis=1)
    pos = (groups[:, None] * GROUP + jnp.arange(GROUP, dtype=jnp.int32)[None, :]).reshape(-1)
    bias = jnp.where(pos[:, None] <= pos[None, :tok], 0.0, NEG_FILL).astype(F32)

    vmem = pl.BlockSpec(memory_space=pltpu.VMEM)
    hbm = pl.BlockSpec(memory_space=pl.ANY)
    total = BLOCKS * BLOCK
    half = total // 2
    pair_shape = jax.ShapeDtypeStruct((PAIRS, total, 2 * tok), BF16)
    latent_shape = jax.ShapeDtypeStruct((half, WIDTH), BF16)
    probs, grads, latent_send = pl.pallas_call(
        scores_kernel,
        grid=(PAIRS + BLOCKS // 2,),
        out_shape=(pair_shape, pair_shape, latent_shape),
        in_specs=[vmem] * (BLOCKS + 3),
        out_specs=(hbm, hbm, pl.BlockSpec((BLOCK, WIDTH), lambda i: (jnp.maximum(i - PAIRS, 0), 0))),
        scratch_shapes=[
            pltpu.VMEM((PAIRS, total, 2 * tok), BF16),
            pltpu.VMEM((PAIRS, total, 2 * tok), BF16),
            pltpu.VMEM((total, 2 * tok), F32),
            pltpu.VMEM((total, 2 * tok), F32),
            pltpu.SemaphoreType.DMA((2, PAIRS)),
        ],
        name="scores",
    )(*k_blocks, query_all, grad_lat, bias)

    latent_got = swap_ctx(latent_send, 1)

    latent_keep = pl.pallas_call(
        keep_kernel,
        grid=(BLOCKS // 2,),
        out_shape=latent_shape,
        in_specs=[
            pl.BlockSpec((PAIRS, BLOCK, 2 * tok), lambda i: (0, i, 0)),
            pl.BlockSpec((PAIRS, BLOCK, 2 * tok), lambda i: (0, i, 0)),
            vmem,
            vmem,
        ],
        out_specs=pl.BlockSpec((BLOCK, WIDTH), lambda i: (i, 0)),
        name="keep",
    )(probs, grads, query_all, grad_lat)

    share = D_LATENT // CTX
    pair_cols = 2 * (NOPE + ROPE)
    weight_shape = jax.ShapeDtypeStruct((CTX // 2, 2, share, heads * NOPE), BF16)
    weight_spec = pl.BlockSpec((CTX // 2, 2, share, 2 * NOPE), lambda i: (0, 0, 0, i))
    query_grad, weight_send, weight_keep = pl.pallas_call(
        weights_kernel,
        grid=(PAIRS,),
        out_shape=(jax.ShapeDtypeStruct(queries.shape, BF16), weight_shape, weight_shape),
        in_specs=[pl.BlockSpec(memory_space=pltpu.SMEM)]
        + [vmem] * BLOCKS
        + [
            pl.BlockSpec((None, total, 2 * tok), lambda i: (i, 0, 0)),
            pl.BlockSpec((None, total, 2 * tok), lambda i: (i, 0, 0)),
            pl.BlockSpec((tok, pair_cols), lambda i: (0, i)),
            pl.BlockSpec((tok, 2 * VDIM), lambda i: (0, i)),
            pl.BlockSpec((D_LATENT, 2 * NOPE), lambda i: (0, i)),
        ],
        out_specs=(pl.BlockSpec((tok, pair_cols), lambda i: (0, i)), weight_spec, weight_spec),
        scratch_shapes=[
            pltpu.VMEM((WIDTH, total), BF16),
            pltpu.VMEM((2, D_LATENT, 2 * NOPE), BF16),
        ],
        name="weights",
    )(own.reshape(1), *k_blocks, probs, grads, queries, out_grad, up_key_weight)

    step = 2 * tok
    pieces = [
        spread_sum([latent_keep[k * step : (k + 1) * step], latent_got[k * step : (k + 1) * step]]).astype(BF16)
        for k in range(4)
    ]
    got = [pieces[0]] + [swap_ctx(pieces[k], k << 2) for k in (1, 2, 3)]
    mine = spread_sum([g[:tok] for g in got]).astype(BF16)
    other = spread_sum([g[tok:] for g in got]).astype(BF16)
    mine = spread_sum([mine, swap_ctx(other, 2)]).astype(BF16)
    mine = spread_sum([mine, swap_head(mine, 1)]).astype(BF16)
    mine = spread_sum([mine, swap_head(mine, 2)]).astype(BF16)
    mine = spread_sum([mine, swap_head(mine, 6)])
    latent_grad, rope_grad = mine[:, :D_LATENT], mine[:, D_LATENT:]

    weight_got = swap_ctx(weight_send, 1)
    pieces = [
        spread_sum([weight_keep[2 * k : 2 * k + 2], weight_got[2 * k : 2 * k + 2]]).astype(BF16) for k in range(4)
    ]
    got = [pieces[0]] + [swap_ctx(pieces[k], k << 2) for k in (1, 2, 3)]
    mine = spread_sum([g[0] for g in got])
    other = spread_sum([g[1] for g in got]).astype(BF16)
    weights = spread_sum([mine, swap_ctx(other, 2)])
    return query_grad, latent_grad, rope_grad, weights[0], weights[1]


def solution(mesh):
    placed = (
        P("ctx", "head"),
        P("ctx", None),
        P("ctx", None),
        P(None, "head"),
        P(None, "head"),
        P("ctx", "head"),
        P(),
    )
    return jax.shard_map(
        per_device,
        mesh=mesh,
        in_specs=placed,
        out_specs=(
            P("ctx", "head"),
            P("ctx", None),
            P("ctx", None),
            P("ctx", "head"),
            P("ctx", "head"),
        ),
        check_vma=False,
    )
```

```python
import math

import jax
import jax.numpy as jnp
from jax import lax
from jax.experimental import pallas as pl
from jax.experimental.pallas import tpu as pltpu
from jax.sharding import PartitionSpec as P


D_LATENT = 512
ROPE = 64
NOPE = 128
VDIM = 128
WIDTH = D_LATENT + ROPE
GROUP = 64
NEG_FILL = -1e30
SCALE = (NOPE + ROPE) ** -0.5
SCALE_LOG2 = SCALE * math.log2(math.e)

CTX = 16
HEAD = 8
BF16 = jnp.bfloat16
F32 = jnp.float32


def ctx_xor(position):
    core, y_bits, zhi = position >> 3, (position >> 1) & 3, position & 1
    return (y_bits << 2) | (zhi << 1) | core


def swap_ctx(value, mask):
    return lax.ppermute(value, "ctx", [(i, i ^ mask) for i in range(CTX)])


def swap_head(value, mask):
    return lax.ppermute(value, "head", [(i, i ^ mask) for i in range(HEAD)])


def dot(a, b, dims):
    return lax.dot_general(a, b, (dims, ((), ())), preferred_element_type=F32)


NT = ((1,), (1,))
NN = ((1,), (0,))
TN = ((0,), (0,))

BLOCK = 256
BLOCKS = 8
PAIRS = 4
CHUNK = 128
ROPE_ROWS = 16
PACKED = CHUNK + ROPE_ROWS
LANES = 128


def load_keys(k_refs, keys, ropes, sems):
    copies = []
    for b in range(BLOCKS):
        for c in range(2):
            chunk = 2 * b + c
            rows = slice(chunk * CHUNK, (chunk + 1) * CHUNK)
            top = c * PACKED
            copies.append(pltpu.make_async_copy(k_refs[b].at[top : top + CHUNK], keys.at[rows, :D_LATENT], sems.at[0, chunk]))
            copies.append(pltpu.make_async_copy(k_refs[b].at[top + CHUNK : top + PACKED], ropes.at[chunk], sems.at[1, chunk]))
    for copy in copies:
        copy.start()
    for copy in copies:
        copy.wait()


def rope_rows(packed):
    return jnp.concatenate([packed[:, g * LANES : (g + 1) * LANES] for g in range(ROPE // ROPE_ROWS)], axis=0)


def prep_kernel(own_ref, order_ref, query_ref, up_key_ref, out_grad_ref, up_value_ref, q_ref, gl_ref, bias_ref):
    queries = query_ref[...]
    step = pl.program_id(0)
    for h in range(2):
        first = h * (NOPE + ROPE)
        cols = slice(h * NOPE, (h + 1) * NOPE)
        rows = slice(h * CHUNK, (h + 1) * CHUNK)
        q_ref[0, rows, :D_LATENT] = dot(queries[:, first : first + NOPE], up_key_ref[:, cols], NT).astype(BF16)
        q_ref[0, rows, D_LATENT:] = queries[:, first + NOPE : first + NOPE + ROPE]
        gl_ref[0, rows, :] = dot(out_grad_ref[:, cols], up_value_ref[:, cols], NT).astype(BF16)
    own = own_ref[0]
    lane = lax.broadcasted_iota(jnp.int32, (GROUP, CHUNK), 1)
    row = lax.broadcasted_iota(jnp.int32, (GROUP, CHUNK), 0)
    query_pos = jnp.where(lane < GROUP, order_ref[2 * own] * GROUP, order_ref[2 * own + 1] * GROUP - GROUP) + lane
    for c in range(CTX // PAIRS):
        position = step * (CTX // PAIRS) + c
        core, y_bits, zhi = position >> 3, (position >> 1) & 3, position & 1
        device = own ^ ((y_bits << 2) | (zhi << 1) | core)
        for g in range(2):
            key_pos = order_ref[2 * device + g] * GROUP + row
            first = c * CHUNK + g * GROUP
            bias_ref[first : first + GROUP, :] = jnp.where(key_pos <= query_pos, 0.0, NEG_FILL).astype(F32)


def latent_rows(probs, grads, q_ref, gl_ref):
    query = q_ref[...].reshape(PAIRS * 2 * CHUNK, WIDTH)
    grad_lat = gl_ref[...].reshape(PAIRS * 2 * CHUNK, D_LATENT)
    both = dot(grads, query, NN)
    return both[:, :D_LATENT] + dot(probs, grad_lat, NN), both[:, D_LATENT:]


def store_latents(out_ref, latent, rope):
    for c in range(latent.shape[0] // CHUNK):
        rows = slice(c * CHUNK, (c + 1) * CHUNK)
        top = c * PACKED
        out_ref[top : top + CHUNK, :] = latent[rows].astype(BF16)
        turned = rope[rows].T
        packed = [turned[g * ROPE_ROWS : (g + 1) * ROPE_ROWS] for g in range(ROPE // ROPE_ROWS)]
        out_ref[top + CHUNK : top + PACKED, :] = jnp.concatenate(packed, axis=1).astype(BF16)


def scores_kernel(*refs):
    k_refs = refs[:BLOCKS]
    q_ref, gl_ref, bias_ref = refs[BLOCKS : BLOCKS + 3]
    probs, grads, send_ref = refs[BLOCKS + 3 : BLOCKS + 6]
    keys, ropes, e_ref, g_ref, key_sems = refs[BLOCKS + 6 :]
    step = pl.program_id(0)

    @pl.when(step == 0)
    def _():
        load_keys(k_refs, keys, ropes, key_sems)
        for chunk in range(CTX):
            keys[chunk * CHUNK : (chunk + 1) * CHUNK, D_LATENT:] = rope_rows(ropes[chunk]).T

    @pl.when(step < PAIRS)
    def _():
        q = q_ref[step]
        gl = gl_ref[step]
        run_max, run_sum, run_dot = None, None, None
        maxes = []
        for kb in range(BLOCKS):
            rows = slice(kb * BLOCK, (kb + 1) * BLOCK)
            block = keys[rows, :]
            s = dot(block, q, NT)
            g = dot(block[:, :D_LATENT], gl, NT)
            bias = bias_ref[rows, :]
            s = s * SCALE_LOG2 + jnp.concatenate([bias, bias], axis=1)
            top = jnp.max(s, axis=0, keepdims=True)
            if kb > 0:
                top = jnp.maximum(run_max, top)
            e = jnp.exp2(s - top)
            part = jnp.sum(e, axis=0, keepdims=True)
            part_dot = jnp.sum(e * g, axis=0, keepdims=True)
            if kb > 0:
                shrink = jnp.exp2(run_max - top)
                part = run_sum * shrink + part
                part_dot = run_dot * shrink + part_dot
            run_max, run_sum, run_dot = top, part, part_dot
            maxes.append(top)
            e_ref[rows, :] = e
            g_ref[rows, :] = g
        inverse = 1.0 / run_sum
        delta = run_dot * inverse
        for kb in range(BLOCKS):
            rows = slice(kb * BLOCK, (kb + 1) * BLOCK)
            factor = jnp.exp2(maxes[kb] - run_max) * inverse
            p = e_ref[rows, :] * factor
            probs[step, rows, :] = p.astype(BF16)
            grads[step, rows, :] = (p * (g_ref[rows, :] - delta) * SCALE).astype(BF16)

    @pl.when(step == PAIRS)
    def _():
        rows = slice((BLOCKS // 2) * BLOCK, BLOCKS * BLOCK)
        both = [jnp.concatenate([ref[i, rows, :] for i in range(PAIRS)], axis=1) for ref in (probs, grads)]
        store_latents(send_ref, *latent_rows(*both, q_ref, gl_ref))


def keep_kernel(probs_ref, grads_ref, q_ref, gl_ref, keep_ref):
    rows = slice(0, (BLOCKS // 2) * BLOCK)
    both = [jnp.concatenate([ref[i, rows, :] for i in range(PAIRS)], axis=1) for ref in (probs_ref, grads_ref)]
    store_latents(keep_ref, *latent_rows(*both, q_ref, gl_ref))


def weights_kernel(*refs):
    own_ref = refs[0]
    k_refs = refs[1 : BLOCKS + 1]
    probs_ref, grads_ref, query_ref, out_grad_ref, up_key_ref = refs[BLOCKS + 1 : BLOCKS + 6]
    query_grad_ref, send_ref, keep_ref = refs[BLOCKS + 6 : BLOCKS + 9]
    keys, ropes, kt_ref, w_ref, key_sems = refs[BLOCKS + 9 :]

    @pl.when(pl.program_id(0) == 0)
    def _():
        load_keys(k_refs, keys, ropes, key_sems)
        for chunk in range(CTX):
            cols = slice(chunk * CHUNK, (chunk + 1) * CHUNK)
            kt_ref[:D_LATENT, cols] = keys[cols, :].T
            kt_ref[D_LATENT:, cols] = rope_rows(ropes[chunk])

    step = pl.program_id(0)
    out_t = dot(kt_ref[:D_LATENT, :], probs_ref[step], NN).astype(BF16)
    abs_t = dot(kt_ref[...], grads_ref[step], NN)
    rope_t = abs_t[D_LATENT:, :]
    abs_t = abs_t[:D_LATENT, :].astype(BF16)
    queries = query_ref[...]
    pieces = []
    for h in range(2):
        cols = slice(h * NOPE, (h + 1) * NOPE)
        first = h * (NOPE + ROPE)
        nope = queries[:, first : first + NOPE]
        w_ref[0, :, cols] = dot(abs_t[:, cols], nope, NN).astype(BF16)
        w_ref[1, :, cols] = dot(out_t[:, cols], out_grad_ref[:, cols], NN).astype(BF16)
        pieces.append(dot(abs_t[:, cols], up_key_ref[:, cols], TN))
        pieces.append(rope_t[:, cols].T)
    query_grad_ref[...] = jnp.concatenate(pieces, axis=1).astype(BF16)
    own = own_ref[0]
    share = D_LATENT // CTX
    for position in range(CTX):
        rows = pl.ds(pl.multiple_of((own ^ ctx_xor(position)) * share, share), share)
        out = send_ref if position >= CTX // 2 else keep_ref
        out[position % (CTX // 2), 0] = w_ref[0, rows, :]
        out[position % (CTX // 2), 1] = w_ref[1, rows, :]


def spread_sum(parts):
    total = parts[0].astype(F32)
    for part in parts[1:]:
        total = total + part.astype(F32)
    return total


def in_hbm(*arrays):
    return [pltpu.with_memory_space_constraint(a, pltpu.HBM) for a in arrays]


def in_vmem(*arrays):
    return [pltpu.with_memory_space_constraint(a, pltpu.VMEM) for a in arrays]


def cost(flops, moved):
    return pl.CostEstimate(flops=flops, transcendentals=0, bytes_accessed=moved)


def per_device(queries, latents, rope_key, up_key_weight, up_value_weight, out_grad, group_order):
    tok = queries.shape[0]
    heads = up_key_weight.shape[1] // NOPE
    own = lax.axis_index("ctx").astype(jnp.int32)
    vmem = pl.BlockSpec(memory_space=pltpu.VMEM)
    smem = pl.BlockSpec(memory_space=pltpu.SMEM)
    hbm = pl.BlockSpec(memory_space=pl.ANY)
    total = BLOCKS * BLOCK
    half = (CTX // 2) * PACKED
    pair_cols = 2 * (NOPE + ROPE)
    rope_parts = ROPE // ROPE_ROWS

    turned = rope_key.T
    packed = jnp.concatenate([turned[g * ROPE_ROWS : (g + 1) * ROPE_ROWS] for g in range(rope_parts)], axis=1)
    keys = jnp.concatenate([latents, packed], axis=0)
    got = swap_ctx(keys, 2)
    keys = jnp.concatenate([keys, got], axis=0)
    near = [keys]
    for k in (2, 1, 3):
        near.append(swap_ctx(keys, k << 2))
    near = [near[0], near[2], near[1], near[3]]
    far = []
    for k in range(4):
        far.append(swap_ctx(near[k], 1))
    k_blocks = near + far

    query_all, grad_lat, bias = pl.pallas_call(
        prep_kernel,
        grid=(PAIRS,),
        out_shape=(
            jax.ShapeDtypeStruct((PAIRS, 2 * tok, WIDTH), BF16),
            jax.ShapeDtypeStruct((PAIRS, 2 * tok, D_LATENT), BF16),
            jax.ShapeDtypeStruct((total, tok), F32),
        ),
        in_specs=[
            smem,
            smem,
            pl.BlockSpec((tok, pair_cols), lambda i: (0, i)),
            pl.BlockSpec((D_LATENT, 2 * NOPE), lambda i: (0, i)),
            pl.BlockSpec((tok, 2 * VDIM), lambda i: (0, i)),
            pl.BlockSpec((D_LATENT, 2 * VDIM), lambda i: (0, i)),
        ],
        out_specs=(
            pl.BlockSpec((1, 2 * tok, WIDTH), lambda i: (i, 0, 0)),
            pl.BlockSpec((1, 2 * tok, D_LATENT), lambda i: (i, 0, 0)),
            pl.BlockSpec((total // PAIRS, tok), lambda i: (i, 0)),
        ),
        compiler_params=pltpu.CompilerParams(vmem_limit_bytes=8 << 20),
        cost_estimate=cost(300_000_000, 10_000_000),
        name="prep",
    )(own.reshape(1), group_order, *in_hbm(queries, up_key_weight, out_grad, up_value_weight))

    pair_shape = pltpu.VMEM((PAIRS, total, 2 * tok), BF16)
    latent_shape = jax.ShapeDtypeStruct((half, D_LATENT), BF16)
    probs, grads, latent_send = pl.pallas_call(
        scores_kernel,
        grid=(PAIRS + 1,),
        out_shape=(pair_shape, pair_shape, latent_shape),
        in_specs=[hbm] * BLOCKS + [vmem] * 3,
        out_specs=(vmem, vmem, vmem),
        scratch_shapes=[
            pltpu.VMEM((total, WIDTH), BF16),
            pltpu.VMEM((CTX, ROPE_ROWS, D_LATENT), BF16),
            pltpu.VMEM((total, 2 * tok), F32),
            pltpu.VMEM((total, 2 * tok), F32),
            pltpu.SemaphoreType.DMA((2, CTX)),
        ],
        compiler_params=pltpu.CompilerParams(vmem_limit_bytes=40 << 20),
        cost_estimate=cost(8_000_000_000, 14_000_000),
        name="scores",
    )(*k_blocks, query_all, grad_lat, bias)

    latent_got = swap_ctx(latent_send, 1)

    latent_keep = pl.pallas_call(
        keep_kernel,
        out_shape=latent_shape,
        in_specs=[vmem] * 4,
        out_specs=vmem,
        compiler_params=pltpu.CompilerParams(vmem_limit_bytes=24 << 20),
        cost_estimate=cost(2_300_000_000, 7_000_000),
        name="keep",
    )(*in_vmem(probs, grads), query_all, grad_lat)

    share = D_LATENT // CTX
    weight_shape = jax.ShapeDtypeStruct((CTX // 2, 2, share, heads * NOPE), BF16)
    weight_spec = pl.BlockSpec((CTX // 2, 2, share, 2 * NOPE), lambda i: (0, 0, 0, i))
    query_grad, weight_send, weight_keep = pl.pallas_call(
        weights_kernel,
        grid=(PAIRS,),
        out_shape=(jax.ShapeDtypeStruct(queries.shape, BF16), weight_shape, weight_shape),
        in_specs=[smem]
        + [hbm] * BLOCKS
        + [
            vmem,
            vmem,
            pl.BlockSpec((tok, pair_cols), lambda i: (0, i)),
            pl.BlockSpec((tok, 2 * VDIM), lambda i: (0, i)),
            pl.BlockSpec((D_LATENT, 2 * NOPE), lambda i: (0, i)),
        ],
        out_specs=(pl.BlockSpec((tok, pair_cols), lambda i: (0, i)), weight_spec, weight_spec),
        scratch_shapes=[
            pltpu.VMEM((total, D_LATENT), BF16),
            pltpu.VMEM((CTX, ROPE_ROWS, D_LATENT), BF16),
            pltpu.VMEM((WIDTH, total), BF16),
            pltpu.VMEM((2, D_LATENT, 2 * NOPE), BF16),
            pltpu.SemaphoreType.DMA((2, CTX)),
        ],
        compiler_params=pltpu.CompilerParams(vmem_limit_bytes=24 << 20),
        cost_estimate=cost(5_000_000_000, 14_000_000),
        name="weights",
    )(own.reshape(1), *k_blocks, *in_vmem(probs, grads), *in_hbm(queries, out_grad, up_key_weight))

    step = 2 * PACKED
    pieces = [
        spread_sum([latent_keep[k * step : (k + 1) * step], latent_got[k * step : (k + 1) * step]]).astype(BF16)
        for k in range(4)
    ]
    got = [pieces[0]]
    for k in (2, 1, 3):
        got.append(swap_ctx(pieces[k], k << 2))
    other = spread_sum([g[PACKED:] for g in got]).astype(BF16)
    other = swap_ctx(other, 2)
    mine = spread_sum([g[:PACKED] for g in got] + [other]).astype(BF16)
    other = swap_head(mine, 1)
    mine = spread_sum([mine, other]).astype(BF16)
    other = swap_head(mine, 2)
    mine = spread_sum([mine, other]).astype(BF16)
    other = swap_head(mine, 6)
    latent_grad = spread_sum([mine[:tok], other[:tok]])
    turned = [
        spread_sum([part[tok:, g * LANES : (g + 1) * LANES] for part in (mine, other)]) for g in range(rope_parts)
    ]
    rope_grad = jnp.concatenate(turned, axis=0).T

    weight_got = swap_ctx(weight_send, 1)
    pieces = [
        spread_sum([weight_keep[2 * k : 2 * k + 2], weight_got[2 * k : 2 * k + 2]]).astype(BF16) for k in range(4)
    ]
    got = [pieces[0]]
    for k in (2, 1, 3):
        got.append(swap_ctx(pieces[k], k << 2))
    other = spread_sum([g[1] for g in got]).astype(BF16)
    other = swap_ctx(other, 2)
    up_key_grad, up_value_grad = (spread_sum([g[0, i] for g in got] + [other[i]]) for i in range(2))
    return query_grad, latent_grad, rope_grad, up_key_grad, up_value_grad


def solution(mesh):
    placed = (
        P("ctx", "head"),
        P("ctx", None),
        P("ctx", None),
        P(None, "head"),
        P(None, "head"),
        P("ctx", "head"),
        P(),
    )
    return jax.shard_map(
        per_device,
        mesh=mesh,
        in_specs=placed,
        out_specs=(
            P("ctx", "head"),
            P("ctx", None),
            P("ctx", None),
            P("ctx", "head"),
            P("ctx", "head"),
        ),
        check_vma=False,
    )
```

```python
import math

import jax
import jax.numpy as jnp
from jax import lax
from jax.experimental import pallas as pl
from jax.experimental.pallas import tpu as pltpu
from jax.sharding import PartitionSpec as P


D_LATENT = 512
ROPE = 64
NOPE = 128
VDIM = 128
WIDTH = D_LATENT + ROPE
GROUP = 64
NEG_FILL = -1e30
SCALE = (NOPE + ROPE) ** -0.5
SCALE_LOG2 = SCALE * math.log2(math.e)

CTX = 16
HEAD = 8
BF16 = jnp.bfloat16
F32 = jnp.float32


def key_xor(position):
    core, zhi, y_bits = position >> 3, (position >> 2) & 1, position & 3
    return (y_bits << 2) | (zhi << 1) | core


def row_xor(position):
    core, y_bits, zhi = position >> 3, (position >> 1) & 3, position & 1
    return (y_bits << 2) | (zhi << 1) | core


def swap_ctx(value, mask):
    return lax.ppermute(value, "ctx", [(i, i ^ mask) for i in range(CTX)])


def swap_head(value, mask):
    return lax.ppermute(value, "head", [(i, i ^ mask) for i in range(HEAD)])


def dot(a, b, dims):
    return lax.dot_general(a, b, (dims, ((), ())), preferred_element_type=F32)


NT = ((1,), (1,))
NN = ((1,), (0,))
TN = ((0,), (0,))

BLOCK = 256
BLOCKS = 8
PAIRS = 4
CHUNK = 128
ROPE_ROWS = 16
PACKED = CHUNK + ROPE_ROWS
LANES = 128
TILE = 64
EARLY = (0, 1, 4, 5)
LATE = (2, 3, 6, 7)


def key_ropes(k_ref):
    return rope_rows(k_ref[CHUNK:, :])


def rope_rows(packed):
    return jnp.concatenate([packed[:, g * LANES : (g + 1) * LANES] for g in range(ROPE // ROPE_ROWS)], axis=0)


def prep_kernel(own_ref, order_ref, query_ref, up_key_ref, out_grad_ref, up_value_ref, q_ref, gl_ref, bias_ref):
    queries = query_ref[...]
    step = pl.program_id(0)
    for h in range(2):
        first = h * (NOPE + ROPE)
        cols = slice(h * NOPE, (h + 1) * NOPE)
        rows = slice(h * CHUNK, (h + 1) * CHUNK)
        q_ref[0, rows, :D_LATENT] = dot(queries[:, first : first + NOPE], up_key_ref[:, cols], NT).astype(BF16)
        q_ref[0, rows, D_LATENT:] = queries[:, first + NOPE : first + NOPE + ROPE]
        gl_ref[0, rows, :] = dot(out_grad_ref[:, cols], up_value_ref[:, cols], NT).astype(BF16)
    own = own_ref[0]
    lane = lax.broadcasted_iota(jnp.int32, (GROUP, CHUNK), 1)
    row = lax.broadcasted_iota(jnp.int32, (GROUP, CHUNK), 0)
    query_pos = jnp.where(lane < GROUP, order_ref[2 * own] * GROUP, order_ref[2 * own + 1] * GROUP - GROUP) + lane
    for c in range(CTX // PAIRS):
        position = step * (CTX // PAIRS) + c
        device = own ^ key_xor(position)
        for g in range(2):
            key_pos = order_ref[2 * device + g] * GROUP + row
            first = c * CHUNK + g * GROUP
            bias_ref[first : first + GROUP, :] = jnp.where(key_pos <= query_pos, 0.0, NEG_FILL).astype(F32)


def latent_rows(probs, grads, q_ref, gl_ref):
    query = q_ref[...].reshape(PAIRS * 2 * CHUNK, WIDTH)
    grad_lat = gl_ref[...].reshape(PAIRS * 2 * CHUNK, D_LATENT)
    both = dot(grads, query, NN) * SCALE
    return both[:, :D_LATENT] + dot(probs, grad_lat, NN), both[:, D_LATENT:]


def store_latents(out_ref, latent, rope):
    for c in range(latent.shape[0] // CHUNK):
        rows = slice(c * CHUNK, (c + 1) * CHUNK)
        top = c * PACKED
        out_ref[top : top + CHUNK, :] = latent[rows].astype(BF16)
        turned = rope[rows].T
        packed = [turned[g * ROPE_ROWS : (g + 1) * ROPE_ROWS] for g in range(ROPE // ROPE_ROWS)]
        out_ref[top + CHUNK : top + PACKED, :] = jnp.concatenate(packed, axis=1).astype(BF16)


def load_keys(k_refs, keys):
    for i, k_ref in enumerate(k_refs):
        rows = slice(i * CHUNK, (i + 1) * CHUNK)
        keys[rows, :D_LATENT] = k_ref[:CHUNK, :]
        keys[rows, D_LATENT:] = key_ropes(k_ref).T


def score_blocks(blocks, step, keys, q_ref, gl_ref, bias_ref, e_ref, g_ref, state):
    q = q_ref[step]
    gl = gl_ref[step]
    tops = []
    for i, kb in enumerate(blocks):
        rows = slice(i * BLOCK, (i + 1) * BLOCK)
        block = keys[rows, :]
        s = dot(block, q, NT)
        g = dot(block[:, :D_LATENT], gl, NT)
        bias = bias_ref[kb * BLOCK : (kb + 1) * BLOCK, :]
        s = s * SCALE_LOG2 + jnp.concatenate([bias, bias], axis=1)
        top = jnp.max(s, axis=0, keepdims=True)
        if state is not None:
            top = jnp.maximum(state[0], top)
        e = jnp.exp2(s - top)
        total = jnp.sum(e, axis=0, keepdims=True)
        weighted = jnp.sum(e * g, axis=0, keepdims=True)
        if state is not None:
            shrink = jnp.exp2(state[0] - top)
            total = state[1] * shrink + total
            weighted = state[2] * shrink + weighted
        state = (top, total, weighted)
        tops.append(top)
        e_ref[rows, :] = e.astype(BF16)
        g_ref[rows, :] = g
    return state, tops


def early_kernel(*refs):
    count = 2 * len(EARLY)
    k_refs = refs[:count]
    q_ref, gl_ref, bias_ref, e_ref, g_ref, state_ref, keys = refs[count:]
    step = pl.program_id(0)

    @pl.when(step == 0)
    def _():
        load_keys(k_refs, keys)

    state, tops = score_blocks(
        EARLY, step, keys, q_ref, gl_ref, bias_ref, e_ref.at[step], g_ref.at[step], None
    )
    for i, value in enumerate(state + tuple(tops)):
        state_ref[step, i : i + 1, :] = value


def scores_kernel(*refs):
    count = 2 * len(LATE)
    k_refs = refs[:count]
    q_ref, gl_ref, bias_ref, early_e, early_g, early_state, probs, grads, send_ref, keys, e_ref, g_ref = refs[count:]
    step = pl.program_id(0)

    @pl.when(step == 0)
    def _():
        load_keys(k_refs, keys)

    @pl.when(step < PAIRS)
    def _():
        before = [early_state[step, i : i + 1, :] for i in range(3 + len(EARLY))]
        state, late_tops = score_blocks(
            LATE, step, keys, q_ref, gl_ref, bias_ref, e_ref, g_ref, tuple(before[:3])
        )
        inverse = 1.0 / state[1]
        delta = state[2] * inverse
        parts = [(EARLY, before[3:], early_e.at[step], early_g.at[step]), (LATE, late_tops, e_ref, g_ref)]
        for blocks, tops, e_part, g_part in parts:
            for i, kb in enumerate(blocks):
                factor = jnp.broadcast_to(jnp.exp2(tops[i] - state[0]) * inverse, (TILE, 2 * CHUNK)).astype(BF16)
                for tile in range(BLOCK // TILE):
                    rows = slice(i * BLOCK + tile * TILE, i * BLOCK + (tile + 1) * TILE)
                    to = slice(kb * BLOCK + tile * TILE, kb * BLOCK + (tile + 1) * TILE)
                    p = e_part[rows, :] * factor
                    probs[step, to, :] = p
                    grads[step, to, :] = p * (g_part[rows, :] - delta).astype(BF16)

    @pl.when(step == PAIRS)
    def _():
        rows = slice((BLOCKS // 2) * BLOCK, BLOCKS * BLOCK)
        both = [jnp.concatenate([ref[i, rows, :] for i in range(PAIRS)], axis=1) for ref in (probs, grads)]
        store_latents(send_ref, *latent_rows(*both, q_ref, gl_ref))


def keep_kernel(probs_ref, grads_ref, q_ref, gl_ref, keep_ref):
    rows = slice(0, (BLOCKS // 2) * BLOCK)
    both = [jnp.concatenate([ref[i, rows, :] for i in range(PAIRS)], axis=1) for ref in (probs_ref, grads_ref)]
    store_latents(keep_ref, *latent_rows(*both, q_ref, gl_ref))


def weights_kernel(*refs):
    own_ref = refs[0]
    k_refs = refs[1 : CTX + 1]
    probs_ref, grads_ref, query_ref, out_grad_ref, up_key_ref = refs[CTX + 1 : CTX + 6]
    query_grad_ref, send_ref, keep_ref, kt_ref, w_ref = refs[CTX + 6 :]
    step = pl.program_id(0)

    @pl.when(step == 0)
    def _():
        for i, k_ref in enumerate(k_refs):
            cols = slice(i * CHUNK, (i + 1) * CHUNK)
            kt_ref[:D_LATENT, cols] = k_ref[:CHUNK, :].T
            kt_ref[D_LATENT:, cols] = key_ropes(k_ref)

    out_t = dot(kt_ref[:D_LATENT, :], probs_ref[step], NN).astype(BF16)
    abs_t = dot(kt_ref[...], grads_ref[step], NN) * SCALE
    rope_t = abs_t[D_LATENT:, :]
    abs_t = abs_t[:D_LATENT, :].astype(BF16)
    queries = query_ref[...]
    pieces = []
    for h in range(2):
        cols = slice(h * NOPE, (h + 1) * NOPE)
        first = h * (NOPE + ROPE)
        nope = queries[:, first : first + NOPE]
        w_ref[0, :, cols] = dot(abs_t[:, cols], nope, NN).astype(BF16)
        w_ref[1, :, cols] = dot(out_t[:, cols], out_grad_ref[:, cols], NN).astype(BF16)
        pieces.append(dot(abs_t[:, cols], up_key_ref[:, cols], TN))
        pieces.append(rope_t[:, cols].T)
    query_grad_ref[...] = jnp.concatenate(pieces, axis=1).astype(BF16)
    own = own_ref[0]
    share = D_LATENT // CTX
    for position in range(CTX):
        rows = pl.ds(pl.multiple_of((own ^ row_xor(position)) * share, share), share)
        out = send_ref if position >= CTX // 2 else keep_ref
        lanes = pl.ds(pl.multiple_of(step * 2 * NOPE, 2 * NOPE), 2 * NOPE)
        out[position % (CTX // 2), 0, :, lanes] = w_ref[0, rows, :]
        out[position % (CTX // 2), 1, :, lanes] = w_ref[1, rows, :]


def spread_sum(parts):
    total = parts[0].astype(F32)
    for part in parts[1:]:
        total = total + part.astype(F32)
    return total


def in_hbm(*arrays):
    return [pltpu.with_memory_space_constraint(a, pltpu.HBM) for a in arrays]


def in_vmem(*arrays):
    return [pltpu.with_memory_space_constraint(a, pltpu.VMEM) for a in arrays]


def cost(flops, moved):
    return pl.CostEstimate(flops=flops, transcendentals=0, bytes_accessed=moved)


def per_device(queries, latents, rope_key, up_key_weight, up_value_weight, out_grad, group_order):
    tok = queries.shape[0]
    heads = up_key_weight.shape[1] // NOPE
    own = lax.axis_index("ctx").astype(jnp.int32)
    vmem = pl.BlockSpec(memory_space=pltpu.VMEM)
    smem = pl.BlockSpec(memory_space=pltpu.SMEM)
    total = BLOCKS * BLOCK
    half = (CTX // 2) * PACKED
    pair_cols = 2 * (NOPE + ROPE)
    rope_parts = ROPE // ROPE_ROWS

    turned = rope_key.T
    packed = jnp.concatenate([turned[g * ROPE_ROWS : (g + 1) * ROPE_ROWS] for g in range(rope_parts)], axis=1)
    keys = jnp.concatenate([latents, packed], axis=0)
    other = swap_ctx(keys, 2)
    k_chunks = [None] * CTX
    for z, chunk in enumerate((keys, other)):
        near = [chunk]
        for k in (1, 2, 3):
            near.append(swap_ctx(chunk, k << 2))
        for k in range(4):
            k_chunks[4 * z + k] = near[k]
            k_chunks[8 + 4 * z + k] = swap_ctx(near[k], 1)

    query_all, grad_lat, bias = pl.pallas_call(
        prep_kernel,
        grid=(PAIRS,),
        out_shape=(
            jax.ShapeDtypeStruct((PAIRS, 2 * tok, WIDTH), BF16),
            jax.ShapeDtypeStruct((PAIRS, 2 * tok, D_LATENT), BF16),
            jax.ShapeDtypeStruct((total, tok), F32),
        ),
        in_specs=[
            smem,
            smem,
            pl.BlockSpec((tok, pair_cols), lambda i: (0, i)),
            pl.BlockSpec((D_LATENT, 2 * NOPE), lambda i: (0, i)),
            pl.BlockSpec((tok, 2 * VDIM), lambda i: (0, i)),
            pl.BlockSpec((D_LATENT, 2 * VDIM), lambda i: (0, i)),
        ],
        out_specs=(
            pl.BlockSpec((1, 2 * tok, WIDTH), lambda i: (i, 0, 0)),
            pl.BlockSpec((1, 2 * tok, D_LATENT), lambda i: (i, 0, 0)),
            pl.BlockSpec((total // PAIRS, tok), lambda i: (i, 0)),
        ),
        compiler_params=pltpu.CompilerParams(vmem_limit_bytes=8 << 20),
        cost_estimate=cost(300_000_000, 10_000_000),
        name="prep",
    )(own.reshape(1), group_order, *in_hbm(queries, up_key_weight, out_grad, up_value_weight))

    pair_shape = pltpu.VMEM((PAIRS, total, 2 * tok), BF16)
    latent_shape = pltpu.VMEM((half, D_LATENT), BF16)
    early_chunks = [k_chunks[2 * kb + c] for kb in EARLY for c in range(2)]
    late_chunks = [k_chunks[2 * kb + c] for kb in LATE for c in range(2)]
    early = len(EARLY) * BLOCK
    late = len(LATE) * BLOCK
    early_parts = pl.pallas_call(
        early_kernel,
        grid=(PAIRS,),
        out_shape=(
            pltpu.VMEM((PAIRS, early, 2 * tok), BF16),
            pltpu.VMEM((PAIRS, early, 2 * tok), F32),
            pltpu.VMEM((PAIRS, 8, 2 * tok), F32),
        ),
        in_specs=[vmem] * (len(early_chunks) + 3),
        out_specs=(vmem,) * 3,
        scratch_shapes=[pltpu.VMEM((early, WIDTH), BF16)],
        compiler_params=pltpu.CompilerParams(vmem_limit_bytes=16 << 20),
        cost_estimate=cost(3_000_000_000, 10_000_000),
        name="early",
    )(*in_vmem(*early_chunks, query_all, grad_lat, bias))
    probs, grads, latent_send = pl.pallas_call(
        scores_kernel,
        grid=(PAIRS + 1,),
        out_shape=(pair_shape, pair_shape, latent_shape),
        in_specs=[vmem] * (len(late_chunks) + 6),
        out_specs=(vmem,) * 3,
        scratch_shapes=[
            pltpu.VMEM((late, WIDTH), BF16),
            pltpu.VMEM((late, 2 * tok), BF16),
            pltpu.VMEM((late, 2 * tok), F32),
        ],
        compiler_params=pltpu.CompilerParams(vmem_limit_bytes=24 << 20),
        cost_estimate=cost(6_000_000_000, 14_000_000),
        name="scores",
    )(*in_vmem(*late_chunks, query_all, grad_lat, bias, *early_parts))

    latent_got = swap_ctx(latent_send, 1)

    latent_keep = pl.pallas_call(
        keep_kernel,
        out_shape=latent_shape,
        in_specs=[vmem] * 4,
        out_specs=vmem,
        compiler_params=pltpu.CompilerParams(vmem_limit_bytes=24 << 20),
        cost_estimate=cost(2_300_000_000, 7_000_000),
        name="keep",
    )(*in_vmem(probs, grads, query_all, grad_lat))

    share = D_LATENT // CTX
    weight_shape = pltpu.VMEM((CTX // 2, 2, share, heads * NOPE), BF16)
    query_grad, weight_send, weight_keep = pl.pallas_call(
        weights_kernel,
        grid=(PAIRS,),
        out_shape=(jax.ShapeDtypeStruct(queries.shape, BF16), weight_shape, weight_shape),
        in_specs=[smem]
        + [vmem] * (CTX + 2)
        + [
            pl.BlockSpec((tok, pair_cols), lambda i: (0, i)),
            pl.BlockSpec((tok, 2 * VDIM), lambda i: (0, i)),
            pl.BlockSpec((D_LATENT, 2 * NOPE), lambda i: (0, i)),
        ],
        out_specs=(pl.BlockSpec((tok, pair_cols), lambda i: (0, i)), vmem, vmem),
        scratch_shapes=[
            pltpu.VMEM((WIDTH, total), BF16),
            pltpu.VMEM((2, D_LATENT, 2 * NOPE), BF16),
        ],
        compiler_params=pltpu.CompilerParams(vmem_limit_bytes=24 << 20),
        cost_estimate=cost(5_000_000_000, 14_000_000),
        name="weights",
    )(own.reshape(1), *in_vmem(*k_chunks, probs, grads), *in_hbm(queries, out_grad, up_key_weight))

    pieces = [
        [
            spread_sum([part[(4 * z + k) * PACKED : (4 * z + k + 1) * PACKED] for part in (latent_keep, latent_got)])
            for z in range(2)
        ]
        for k in range(4)
    ]
    pieces = [jnp.concatenate(p, axis=0).astype(BF16) for p in pieces]
    got = [pieces[0]]
    for k in (2, 1, 3):
        got.append(swap_ctx(pieces[k], k << 2))
    other = spread_sum([g[PACKED:] for g in got]).astype(BF16)
    other = swap_ctx(other, 2)
    mine = spread_sum([g[:PACKED] for g in got] + [other]).astype(BF16)
    other = swap_head(mine, 1)
    mine = spread_sum([mine, other]).astype(BF16)
    other = swap_head(mine, 2)
    mine = spread_sum([mine, other]).astype(BF16)
    other = swap_head(mine, 6)
    latent_grad = spread_sum([mine[:tok], other[:tok]])
    turned = [
        spread_sum([part[tok:, g * LANES : (g + 1) * LANES] for part in (mine, other)]) for g in range(rope_parts)
    ]
    rope_grad = jnp.concatenate(turned, axis=0).T

    weight_got = swap_ctx(weight_send, 1)
    pieces = [
        spread_sum([weight_keep[2 * k : 2 * k + 2], weight_got[2 * k : 2 * k + 2]]).astype(BF16) for k in range(4)
    ]
    got = [pieces[0]]
    for k in (2, 1, 3):
        got.append(swap_ctx(pieces[k], k << 2))
    other = spread_sum([g[1] for g in got]).astype(BF16)
    other = swap_ctx(other, 2)
    up_key_grad, up_value_grad = (spread_sum([g[0, i] for g in got] + [other[i]]) for i in range(2))
    return query_grad, latent_grad, rope_grad, up_key_grad, up_value_grad


def solution(mesh):
    placed = (
        P("ctx", "head"),
        P("ctx", None),
        P("ctx", None),
        P(None, "head"),
        P(None, "head"),
        P("ctx", "head"),
        P(),
    )
    return jax.shard_map(
        per_device,
        mesh=mesh,
        in_specs=placed,
        out_specs=(
            P("ctx", "head"),
            P("ctx", None),
            P("ctx", None),
            P("ctx", "head"),
            P("ctx", "head"),
        ),
        check_vma=False,
    )
```

```python
import math

import jax
import jax.numpy as jnp
from jax import lax
from jax.experimental import pallas as pl
from jax.experimental.pallas import tpu as pltpu
from jax.sharding import PartitionSpec as P


D_LATENT = 512
ROPE = 64
NOPE = 128
VDIM = 128
WIDTH = D_LATENT + ROPE
GROUP = 64
NEG_FILL = -1e30
SCALE = (NOPE + ROPE) ** -0.5
SCALE_LOG2 = SCALE * math.log2(math.e)

CTX = 16
HEAD = 8
BF16 = jnp.bfloat16
F32 = jnp.float32


def key_xor(position):
    core, zhi, y_bits = position >> 3, (position >> 2) & 1, position & 3
    return (y_bits << 2) | (zhi << 1) | core


def row_xor(position):
    core, y_bits, zhi = position >> 3, (position >> 1) & 3, position & 1
    return (y_bits << 2) | (zhi << 1) | core


def swap_ctx(value, mask):
    return lax.ppermute(value, "ctx", [(i, i ^ mask) for i in range(CTX)])


def swap_head(value, mask):
    return lax.ppermute(value, "head", [(i, i ^ mask) for i in range(HEAD)])


def swap_both(value, ctx_mask, head_mask):
    mask = ctx_mask * HEAD + head_mask
    return lax.ppermute(value, ("ctx", "head"), [(i, i ^ mask) for i in range(CTX * HEAD)])


def dot(a, b, dims):
    return lax.dot_general(a, b, (dims, ((), ())), preferred_element_type=F32)


NT = ((1,), (1,))
NN = ((1,), (0,))
TN = ((0,), (0,))

BLOCK = 256
BLOCKS = 8
PAIRS = 4
CHUNK = 128
ROPE_ROWS = 16
PACKED = CHUNK + ROPE_ROWS
LANES = 128
PAIR_COLS = 2 * (NOPE + ROPE)
TILE = 64
EARLY = (0, 1, 4, 5)
LATE = (2, 3, 6, 7)


def key_ropes(k_ref):
    return rope_rows(k_ref[CHUNK:, :])


def rope_rows(packed):
    return jnp.concatenate([packed[:, g * LANES : (g + 1) * LANES] for g in range(ROPE // ROPE_ROWS)], axis=0)


def pack_kernel(latents_ref, turned_ref, out_ref):
    out_ref[:CHUNK, :] = latents_ref[...]
    for g in range(ROPE // ROPE_ROWS):
        out_ref[CHUNK:, g * LANES : (g + 1) * LANES] = turned_ref[g * ROPE_ROWS : (g + 1) * ROPE_ROWS, :]


def prep_kernel(own_ref, order_ref, query_ref, up_key_ref, out_grad_ref, up_value_ref, q_ref, gl_ref, bias_ref):
    queries = query_ref[...]
    step = pl.program_id(0)
    for h in range(2):
        first = h * (NOPE + ROPE)
        cols = slice(h * NOPE, (h + 1) * NOPE)
        rows = slice(h * CHUNK, (h + 1) * CHUNK)
        q_ref[0, rows, :D_LATENT] = dot(queries[:, first : first + NOPE], up_key_ref[:, cols], NT).astype(BF16)
        q_ref[0, rows, D_LATENT:] = queries[:, first + NOPE : first + NOPE + ROPE]
        gl_ref[0, rows, :] = dot(out_grad_ref[:, cols], up_value_ref[:, cols], NT).astype(BF16)
    own = own_ref[0]
    lane = lax.broadcasted_iota(jnp.int32, (GROUP, CHUNK), 1)
    row = lax.broadcasted_iota(jnp.int32, (GROUP, CHUNK), 0)
    query_pos = jnp.where(lane < GROUP, order_ref[2 * own] * GROUP, order_ref[2 * own + 1] * GROUP - GROUP) + lane
    for c in range(CTX // PAIRS):
        position = step * (CTX // PAIRS) + c
        device = own ^ key_xor(position)
        for g in range(2):
            key_pos = order_ref[2 * device + g] * GROUP + row
            first = c * CHUNK + g * GROUP
            bias_ref[first : first + GROUP, :] = jnp.where(key_pos <= query_pos, 0.0, NEG_FILL).astype(F32)


def latent_rows(probs, grads, q_ref, gl_ref):
    query = q_ref[...].reshape(PAIRS * 2 * CHUNK, WIDTH)
    grad_lat = gl_ref[...].reshape(PAIRS * 2 * CHUNK, D_LATENT)
    both = dot(grads, query, NN) * SCALE
    return both[:, :D_LATENT] + dot(probs, grad_lat, NN), both[:, D_LATENT:]


def store_latents(out_ref, latent, rope):
    for c in range(latent.shape[0] // CHUNK):
        rows = slice(c * CHUNK, (c + 1) * CHUNK)
        top = c * PACKED
        out_ref[top : top + CHUNK, :] = latent[rows].astype(BF16)
        turned = rope[rows].T
        packed = [turned[g * ROPE_ROWS : (g + 1) * ROPE_ROWS] for g in range(ROPE // ROPE_ROWS)]
        out_ref[top + CHUNK : top + PACKED, :] = jnp.concatenate(packed, axis=1).astype(BF16)


def load_keys(k_refs, keys):
    for i, k_ref in enumerate(k_refs):
        rows = slice(i * CHUNK, (i + 1) * CHUNK)
        keys[rows, :D_LATENT] = k_ref[:CHUNK, :]
        keys[rows, D_LATENT:] = key_ropes(k_ref).T


def score_blocks(blocks, step, keys, q_ref, gl_ref, bias_ref, e_ref, g_ref, state):
    q = q_ref[step]
    gl = gl_ref[step]
    tops = []
    for i, kb in enumerate(blocks):
        rows = slice(i * BLOCK, (i + 1) * BLOCK)
        block = keys[rows, :]
        s = dot(block, q, NT)
        g = dot(block[:, :D_LATENT], gl, NT)
        bias = bias_ref[kb * BLOCK : (kb + 1) * BLOCK, :]
        s = s * SCALE_LOG2 + jnp.concatenate([bias, bias], axis=1)
        top = jnp.max(s, axis=0, keepdims=True)
        if state is not None:
            top = jnp.maximum(state[0], top)
        e = jnp.exp2(s - top)
        total = jnp.sum(e, axis=0, keepdims=True)
        weighted = jnp.sum(e * g, axis=0, keepdims=True)
        if state is not None:
            shrink = jnp.exp2(state[0] - top)
            total = state[1] * shrink + total
            weighted = state[2] * shrink + weighted
        state = (top, total, weighted)
        tops.append(top)
        e_ref[rows, :] = e.astype(BF16)
        g_ref[rows, :] = g
    return state, tops


def early_kernel(*refs):
    count = 2 * len(EARLY)
    k_refs = refs[:count]
    q_ref, gl_ref, bias_ref, e_ref, g_ref, state_ref, keys = refs[count:]
    step = pl.program_id(0)

    @pl.when(step == 0)
    def _():
        load_keys(k_refs, keys)

    state, tops = score_blocks(
        EARLY, step, keys, q_ref, gl_ref, bias_ref, e_ref.at[step], g_ref.at[step], None
    )
    for i, value in enumerate(state + tuple(tops)):
        state_ref[step, i : i + 1, :] = value


def scores_kernel(*refs):
    count = 2 * len(LATE)
    k_refs = refs[:count]
    q_ref, gl_ref, bias_ref, early_e, early_g, early_state, probs, grads, send_ref, keys, e_ref, g_ref = refs[count:]
    step = pl.program_id(0)

    @pl.when(step == 0)
    def _():
        load_keys(k_refs, keys)

    @pl.when(step < PAIRS)
    def _():
        before = [early_state[step, i : i + 1, :] for i in range(3 + len(EARLY))]
        state, late_tops = score_blocks(
            LATE, step, keys, q_ref, gl_ref, bias_ref, e_ref, g_ref, tuple(before[:3])
        )
        inverse = 1.0 / state[1]
        delta = state[2] * inverse
        parts = [(EARLY, before[3:], early_e.at[step], early_g.at[step]), (LATE, late_tops, e_ref, g_ref)]
        for blocks, tops, e_part, g_part in parts:
            for i, kb in enumerate(blocks):
                factor = jnp.broadcast_to(jnp.exp2(tops[i] - state[0]) * inverse, (TILE, 2 * CHUNK)).astype(BF16)
                for tile in range(BLOCK // TILE):
                    rows = slice(i * BLOCK + tile * TILE, i * BLOCK + (tile + 1) * TILE)
                    to = slice(kb * BLOCK + tile * TILE, kb * BLOCK + (tile + 1) * TILE)
                    p = e_part[rows, :] * factor
                    probs[step, to, :] = p
                    grads[step, to, :] = p * (g_part[rows, :] - delta).astype(BF16)

    @pl.when(step == PAIRS)
    def _():
        rows = slice((BLOCKS // 2) * BLOCK, BLOCKS * BLOCK)
        both = [jnp.concatenate([ref[i, rows, :] for i in range(PAIRS)], axis=1) for ref in (probs, grads)]
        store_latents(send_ref, *latent_rows(*both, q_ref, gl_ref))


def keep_kernel(probs_ref, grads_ref, q_ref, gl_ref, keep_ref):
    rows = slice(0, (BLOCKS // 2) * BLOCK)
    both = [jnp.concatenate([ref[i, rows, :] for i in range(PAIRS)], axis=1) for ref in (probs_ref, grads_ref)]
    store_latents(keep_ref, *latent_rows(*both, q_ref, gl_ref))


def weights_kernel(*refs):
    own_ref = refs[0]
    k_refs = refs[1 : CTX + 1]
    probs_ref, grads_ref, query_ref, out_grad_ref, up_key_ref = refs[CTX + 1 : CTX + 6]
    query_grad_ref, send_ref, keep_ref, kt_ref, w_ref = refs[CTX + 6 :]
    step = pl.program_id(0)

    @pl.when(step == 0)
    def _():
        for i, k_ref in enumerate(k_refs):
            cols = slice(i * CHUNK, (i + 1) * CHUNK)
            kt_ref[:D_LATENT, cols] = k_ref[:CHUNK, :].T
            kt_ref[D_LATENT:, cols] = key_ropes(k_ref)

    out_t = dot(kt_ref[:D_LATENT, :], probs_ref[step], NN).astype(BF16)
    abs_t = dot(kt_ref[...], grads_ref[step], NN) * SCALE
    rope_t = abs_t[D_LATENT:, :]
    abs_t = abs_t[:D_LATENT, :].astype(BF16)
    queries = query_ref[:, pl.ds(pl.multiple_of(step * PAIR_COLS, PAIR_COLS), PAIR_COLS)]
    lanes = pl.ds(pl.multiple_of(step * 2 * NOPE, 2 * NOPE), 2 * NOPE)
    grad_out = out_grad_ref[:, lanes]
    up_key = up_key_ref[:, lanes]
    pieces = []
    for h in range(2):
        cols = slice(h * NOPE, (h + 1) * NOPE)
        first = h * (NOPE + ROPE)
        nope = queries[:, first : first + NOPE]
        w_ref[0, :, cols] = dot(abs_t[:, cols], nope, NN).astype(BF16)
        w_ref[1, :, cols] = dot(out_t[:, cols], grad_out[:, cols], NN).astype(BF16)
        pieces.append(dot(abs_t[:, cols], up_key[:, cols], TN))
        pieces.append(rope_t[:, cols].T)
    query_grad_ref[...] = jnp.concatenate(pieces, axis=1).astype(BF16)
    own = own_ref[0]
    share = D_LATENT // CTX
    for position in range(CTX):
        rows = pl.ds(pl.multiple_of((own ^ row_xor(position)) * share, share), share)
        out = send_ref if position >= CTX // 2 else keep_ref
        out[position % (CTX // 2), 0, :, lanes] = w_ref[0, rows, :]
        out[position % (CTX // 2), 1, :, lanes] = w_ref[1, rows, :]


def spread_sum(parts):
    total = parts[0].astype(F32)
    for part in parts[1:]:
        total = total + part.astype(F32)
    return total


def in_hbm(*arrays):
    return [pltpu.with_memory_space_constraint(a, pltpu.HBM) for a in arrays]


def in_vmem(*arrays):
    return [pltpu.with_memory_space_constraint(a, pltpu.VMEM) for a in arrays]


def cost(flops, moved):
    return pl.CostEstimate(flops=flops, transcendentals=0, bytes_accessed=moved)


def per_device(queries, latents, rope_key, up_key_weight, up_value_weight, out_grad, group_order):
    tok = queries.shape[0]
    heads = up_key_weight.shape[1] // NOPE
    own = lax.axis_index("ctx").astype(jnp.int32)
    vmem = pl.BlockSpec(memory_space=pltpu.VMEM)
    smem = pl.BlockSpec(memory_space=pltpu.SMEM)
    total = BLOCKS * BLOCK
    half = (CTX // 2) * PACKED
    pair_cols = 2 * (NOPE + ROPE)
    rope_parts = ROPE // ROPE_ROWS

    keys = pl.pallas_call(
        pack_kernel,
        out_shape=pltpu.VMEM((PACKED, D_LATENT), BF16),
        in_specs=[vmem] * 2,
        out_specs=vmem,
        compiler_params=pltpu.CompilerParams(vmem_limit_bytes=4 << 20),
        name="pack",
    )(*in_hbm(latents, rope_key.T))
    other = swap_ctx(keys, 2)
    k_chunks = [None] * CTX
    for z, chunk in enumerate((keys, other)):
        near = [chunk]
        for k in (1, 2, 3):
            near.append(swap_ctx(chunk, k << 2))
        for k in range(4):
            k_chunks[4 * z + k] = near[k]
            k_chunks[8 + 4 * z + k] = swap_ctx(near[k], 1)

    query_all, grad_lat, bias = pl.pallas_call(
        prep_kernel,
        grid=(PAIRS,),
        out_shape=(
            jax.ShapeDtypeStruct((PAIRS, 2 * tok, WIDTH), BF16),
            jax.ShapeDtypeStruct((PAIRS, 2 * tok, D_LATENT), BF16),
            jax.ShapeDtypeStruct((total, tok), F32),
        ),
        in_specs=[
            smem,
            smem,
            pl.BlockSpec((tok, pair_cols), lambda i: (0, i)),
            pl.BlockSpec((D_LATENT, 2 * NOPE), lambda i: (0, i)),
            pl.BlockSpec((tok, 2 * VDIM), lambda i: (0, i)),
            pl.BlockSpec((D_LATENT, 2 * VDIM), lambda i: (0, i)),
        ],
        out_specs=(
            pl.BlockSpec((1, 2 * tok, WIDTH), lambda i: (i, 0, 0)),
            pl.BlockSpec((1, 2 * tok, D_LATENT), lambda i: (i, 0, 0)),
            pl.BlockSpec((total // PAIRS, tok), lambda i: (i, 0)),
        ),
        compiler_params=pltpu.CompilerParams(vmem_limit_bytes=8 << 20),
        cost_estimate=cost(300_000_000, 10_000_000),
        name="prep",
    )(own.reshape(1), *in_hbm(group_order, queries, up_key_weight, out_grad, up_value_weight))

    pair_shape = pltpu.VMEM((PAIRS, total, 2 * tok), BF16)
    latent_shape = pltpu.VMEM((half, D_LATENT), BF16)
    early_chunks = [k_chunks[2 * kb + c] for kb in EARLY for c in range(2)]
    late_chunks = [k_chunks[2 * kb + c] for kb in LATE for c in range(2)]
    early = len(EARLY) * BLOCK
    late = len(LATE) * BLOCK
    early_parts = pl.pallas_call(
        early_kernel,
        grid=(PAIRS,),
        out_shape=(
            pltpu.VMEM((PAIRS, early, 2 * tok), BF16),
            pltpu.VMEM((PAIRS, early, 2 * tok), F32),
            pltpu.VMEM((PAIRS, 8, 2 * tok), F32),
        ),
        in_specs=[vmem] * (len(early_chunks) + 3),
        out_specs=(vmem,) * 3,
        scratch_shapes=[pltpu.VMEM((early, WIDTH), BF16)],
        compiler_params=pltpu.CompilerParams(vmem_limit_bytes=16 << 20),
        cost_estimate=cost(3_000_000_000, 10_000_000),
        name="early",
    )(*in_vmem(*early_chunks, query_all, grad_lat, bias))
    probs, grads, latent_send = pl.pallas_call(
        scores_kernel,
        grid=(PAIRS + 1,),
        out_shape=(pair_shape, pair_shape, latent_shape),
        in_specs=[vmem] * (len(late_chunks) + 6),
        out_specs=(vmem,) * 3,
        scratch_shapes=[
            pltpu.VMEM((late, WIDTH), BF16),
            pltpu.VMEM((late, 2 * tok), BF16),
            pltpu.VMEM((late, 2 * tok), F32),
        ],
        compiler_params=pltpu.CompilerParams(vmem_limit_bytes=24 << 20),
        cost_estimate=cost(6_000_000_000, 14_000_000),
        name="scores",
    )(*in_vmem(*late_chunks, query_all, grad_lat, bias, *early_parts))

    latent_got = swap_ctx(latent_send, 1)

    latent_keep = pl.pallas_call(
        keep_kernel,
        out_shape=latent_shape,
        in_specs=[vmem] * 4,
        out_specs=vmem,
        compiler_params=pltpu.CompilerParams(vmem_limit_bytes=24 << 20),
        cost_estimate=cost(2_300_000_000, 7_000_000),
        name="keep",
    )(*in_vmem(probs, grads, query_all, grad_lat))

    share = D_LATENT // CTX
    weight_shape = pltpu.VMEM((CTX // 2, 2, share, heads * NOPE), BF16)
    query_grad, weight_send, weight_keep = pl.pallas_call(
        weights_kernel,
        grid=(PAIRS,),
        out_shape=(jax.ShapeDtypeStruct(queries.shape, BF16), weight_shape, weight_shape),
        in_specs=[smem]
        + [vmem] * (CTX + 2)
        + [
            vmem,
            vmem,
            vmem,
        ],
        out_specs=(pl.BlockSpec((tok, pair_cols), lambda i: (0, i)), vmem, vmem),
        scratch_shapes=[
            pltpu.VMEM((WIDTH, total), BF16),
            pltpu.VMEM((2, D_LATENT, 2 * NOPE), BF16),
        ],
        compiler_params=pltpu.CompilerParams(vmem_limit_bytes=24 << 20),
        cost_estimate=cost(5_000_000_000, 14_000_000),
        name="weights",
    )(own.reshape(1), *in_vmem(*k_chunks, probs, grads, queries, out_grad, up_key_weight))

    pieces = [
        [
            spread_sum([part[(4 * z + k) * PACKED : (4 * z + k + 1) * PACKED] for part in (latent_keep, latent_got)])
            for z in range(2)
        ]
        for k in range(4)
    ]
    pieces = [jnp.concatenate(p, axis=0).astype(BF16) for p in pieces]
    got = [pieces[0]]
    for k in (2, 1, 3):
        got.append(swap_ctx(pieces[k], k << 2))
    other = spread_sum([g[PACKED:] for g in got]).astype(BF16)
    mine = spread_sum([g[:PACKED] for g in got]).astype(BF16)
    first = swap_ctx(other, 2)
    second = swap_both(other, 2, 1)
    third = swap_head(mine, 1)
    mine = spread_sum([mine, first, second, third])
    mine = mine.astype(BF16)
    other = swap_head(mine, 2)
    mine = spread_sum([mine, other]).astype(BF16)
    other = swap_head(mine, 6)
    latent_grad = spread_sum([mine[:tok], other[:tok]])
    turned = [
        spread_sum([part[tok:, g * LANES : (g + 1) * LANES] for part in (mine, other)]) for g in range(rope_parts)
    ]
    rope_grad = jnp.concatenate(turned, axis=0).T

    weight_got = swap_ctx(weight_send, 1)
    pieces = [
        spread_sum([weight_keep[2 * k : 2 * k + 2], weight_got[2 * k : 2 * k + 2]]).astype(BF16) for k in range(4)
    ]
    got = [pieces[0]]
    for k in (2, 1, 3):
        got.append(swap_ctx(pieces[k], k << 2))
    other = spread_sum([g[1] for g in got]).astype(BF16)
    other = swap_ctx(other, 2)
    up_key_grad, up_value_grad = (spread_sum([g[0, i] for g in got] + [other[i]]) for i in range(2))
    return query_grad, latent_grad, rope_grad, up_key_grad, up_value_grad


def solution(mesh):
    placed = (
        P("ctx", "head"),
        P("ctx", None),
        P("ctx", None),
        P(None, "head"),
        P(None, "head"),
        P("ctx", "head"),
        P(),
    )
    return jax.shard_map(
        per_device,
        mesh=mesh,
        in_specs=placed,
        out_specs=(
            P("ctx", "head"),
            P("ctx", None),
            P("ctx", None),
            P("ctx", "head"),
            P("ctx", "head"),
        ),
        check_vma=False,
    )
```

```python
import math

import jax
import jax.numpy as jnp
from jax import lax
from jax.experimental import pallas as pl
from jax.experimental.pallas import tpu as pltpu
from jax.sharding import PartitionSpec as P


D_LATENT = 512
ROPE = 64
NOPE = 128
VDIM = 128
WIDTH = D_LATENT + ROPE
GROUP = 64
NEG_FILL = -1e30
SCALE = (NOPE + ROPE) ** -0.5
SCALE_LOG2 = SCALE * math.log2(math.e)

CTX = 16
HEAD = 8
BF16 = jnp.bfloat16
F32 = jnp.float32


def key_xor(position):
    core, zhi, y_bits = position >> 3, (position >> 2) & 1, position & 3
    return (y_bits << 2) | (zhi << 1) | core


def row_xor(position):
    core, y_bits, zhi = position >> 3, (position >> 1) & 3, position & 1
    return (y_bits << 2) | (zhi << 1) | core


def swap_ctx(value, mask):
    return lax.ppermute(value, "ctx", [(i, i ^ mask) for i in range(CTX)])


def swap_head(value, mask):
    return lax.ppermute(value, "head", [(i, i ^ mask) for i in range(HEAD)])


def swap_both(value, ctx_mask, head_mask):
    mask = ctx_mask * HEAD + head_mask
    return lax.ppermute(value, ("ctx", "head"), [(i, i ^ mask) for i in range(CTX * HEAD)])


def dot(a, b, dims):
    return lax.dot_general(a, b, (dims, ((), ())), preferred_element_type=F32)


NT = ((1,), (1,))
NN = ((1,), (0,))
TN = ((0,), (0,))

BLOCK = 256
BLOCKS = 8
PAIRS = 4
CHUNK = 128
ROPE_ROWS = 16
PACKED = CHUNK + ROPE_ROWS
LANES = 128
PAIR_COLS = 2 * (NOPE + ROPE)
TILE = 64
EARLY = (0, 1, 4, 5)
LATE = (2, 3, 6, 7)


def key_ropes(k_ref):
    return rope_rows(k_ref[CHUNK:, :])


def rope_rows(packed):
    return jnp.concatenate([packed[:, g * LANES : (g + 1) * LANES] for g in range(ROPE // ROPE_ROWS)], axis=0)


def pack_kernel(latents_ref, turned_ref, out_ref):
    out_ref[:CHUNK, :] = latents_ref[...]
    for g in range(ROPE // ROPE_ROWS):
        out_ref[CHUNK:, g * LANES : (g + 1) * LANES] = turned_ref[g * ROPE_ROWS : (g + 1) * ROPE_ROWS, :]


def final_kernel(mine_ref, other_ref, latent_ref, turned_ref):
    total = mine_ref[...].astype(F32) + other_ref[...].astype(F32)
    latent_ref[...] = total[:CHUNK]
    turned_ref[...] = rope_rows(total[CHUNK:])


def prep_kernel(own_ref, order_ref, query_ref, up_key_ref, out_grad_ref, up_value_ref, q_ref, gl_ref, bias_ref):
    queries = query_ref[...]
    step = pl.program_id(0)
    for h in range(2):
        first = h * (NOPE + ROPE)
        cols = slice(h * NOPE, (h + 1) * NOPE)
        rows = slice(h * CHUNK, (h + 1) * CHUNK)
        q_ref[0, rows, :D_LATENT] = dot(queries[:, first : first + NOPE], up_key_ref[:, cols], NT).astype(BF16)
        q_ref[0, rows, D_LATENT:] = queries[:, first + NOPE : first + NOPE + ROPE]
        gl_ref[0, rows, :] = dot(out_grad_ref[:, cols], up_value_ref[:, cols], NT).astype(BF16)
    own = own_ref[0]
    lane = lax.broadcasted_iota(jnp.int32, (GROUP, CHUNK), 1)
    row = lax.broadcasted_iota(jnp.int32, (GROUP, CHUNK), 0)
    query_pos = jnp.where(lane < GROUP, order_ref[2 * own] * GROUP, order_ref[2 * own + 1] * GROUP - GROUP) + lane
    for c in range(CTX // PAIRS):
        position = step * (CTX // PAIRS) + c
        device = own ^ key_xor(position)
        for g in range(2):
            key_pos = order_ref[2 * device + g] * GROUP + row
            first = c * CHUNK + g * GROUP
            bias_ref[first : first + GROUP, :] = jnp.where(key_pos <= query_pos, 0.0, NEG_FILL).astype(F32)


def latent_rows(probs, grads, q_ref, gl_ref):
    query = q_ref[...].reshape(PAIRS * 2 * CHUNK, WIDTH)
    grad_lat = gl_ref[...].reshape(PAIRS * 2 * CHUNK, D_LATENT)
    both = dot(grads, query, NN) * SCALE
    return both[:, :D_LATENT] + dot(probs, grad_lat, NN), both[:, D_LATENT:]


def store_latents(out_ref, latent, rope):
    for c in range(latent.shape[0] // CHUNK):
        rows = slice(c * CHUNK, (c + 1) * CHUNK)
        top = c * PACKED
        out_ref[top : top + CHUNK, :] = latent[rows].astype(BF16)
        turned = rope[rows].T
        packed = [turned[g * ROPE_ROWS : (g + 1) * ROPE_ROWS] for g in range(ROPE // ROPE_ROWS)]
        out_ref[top + CHUNK : top + PACKED, :] = jnp.concatenate(packed, axis=1).astype(BF16)


def load_keys(k_refs, keys):
    for i, k_ref in enumerate(k_refs):
        rows = slice(i * CHUNK, (i + 1) * CHUNK)
        keys[rows, :D_LATENT] = k_ref[:CHUNK, :]
        keys[rows, D_LATENT:] = key_ropes(k_ref).T


def score_blocks(blocks, step, keys, q_ref, gl_ref, bias_ref, e_ref, g_ref, state):
    q = q_ref[step]
    gl = gl_ref[step]
    tops = []
    for i, kb in enumerate(blocks):
        rows = slice(i * BLOCK, (i + 1) * BLOCK)
        block = keys[rows, :]
        s = dot(block, q, NT)
        g = dot(block[:, :D_LATENT], gl, NT)
        bias = bias_ref[kb * BLOCK : (kb + 1) * BLOCK, :]
        s = s * SCALE_LOG2 + jnp.concatenate([bias, bias], axis=1)
        top = jnp.max(s, axis=0, keepdims=True)
        if state is not None:
            top = jnp.maximum(state[0], top)
        e = jnp.exp2(s - top)
        total = jnp.sum(e, axis=0, keepdims=True)
        weighted = jnp.sum(e * g, axis=0, keepdims=True)
        if state is not None:
            shrink = jnp.exp2(state[0] - top)
            total = state[1] * shrink + total
            weighted = state[2] * shrink + weighted
        state = (top, total, weighted)
        tops.append(top)
        e_ref[rows, :] = e.astype(BF16)
        g_ref[rows, :] = g
    return state, tops


def turn_keys(k_refs, own, turned):
    share = D_LATENT // CTX
    for i, k_ref in enumerate(k_refs):
        cols = slice(i * CHUNK, (i + 1) * CHUNK)
        block = k_ref[:CHUNK, :].T
        for r in range(CTX):
            other = own ^ r
            position = ((other & 1) << 3) | ((other >> 2) << 1) | ((other >> 1) & 1)
            to = pl.ds(pl.multiple_of(position * share, share), share)
            turned[to, cols] = block[r * share : (r + 1) * share, :]
        turned[D_LATENT:, cols] = key_ropes(k_ref)


def early_kernel(*refs):
    count = 2 * len(EARLY)
    k_refs = refs[:count]
    q_ref, gl_ref, bias_ref, e_ref, g_ref, state_ref, keys = refs[count:]
    step = pl.program_id(0)

    @pl.when(step == 0)
    def _():
        load_keys(k_refs, keys)

    state, tops = score_blocks(
        EARLY, step, keys, q_ref, gl_ref, bias_ref, e_ref.at[step], g_ref.at[step], None
    )
    for i, value in enumerate(state + tuple(tops)):
        state_ref[step, i : i + 1, :] = value


def scores_kernel(*refs):
    count = 2 * len(LATE)
    own_ref, k_refs, early_refs = refs[0], refs[1 : count + 1], refs[count + 1 : CTX + 1]
    q_ref, gl_ref, bias_ref, early_e, early_g, early_state = refs[CTX + 1 : CTX + 7]
    probs, grads, send_ref, early_turned, turned, keys, e_ref, g_ref = refs[CTX + 7 :]
    step = pl.program_id(0)

    @pl.when(step == 0)
    def _():
        load_keys(k_refs, keys)

    @pl.when(step < PAIRS)
    def _():
        before = [early_state[step, i : i + 1, :] for i in range(3 + len(EARLY))]
        state, late_tops = score_blocks(
            LATE, step, keys, q_ref, gl_ref, bias_ref, e_ref, g_ref, tuple(before[:3])
        )
        inverse = 1.0 / state[1]
        delta = state[2] * inverse
        parts = [(EARLY, before[3:], early_e.at[step], early_g.at[step]), (LATE, late_tops, e_ref, g_ref)]
        for blocks, tops, e_part, g_part in parts:
            for i, kb in enumerate(blocks):
                factor = jnp.broadcast_to(jnp.exp2(tops[i] - state[0]) * inverse, (TILE, 2 * CHUNK)).astype(BF16)
                for tile in range(BLOCK // TILE):
                    rows = slice(i * BLOCK + tile * TILE, i * BLOCK + (tile + 1) * TILE)
                    to = slice(kb * BLOCK + tile * TILE, kb * BLOCK + (tile + 1) * TILE)
                    p = e_part[rows, :] * factor
                    probs[step, to, :] = p
                    grads[step, to, :] = p * (g_part[rows, :] - delta).astype(BF16)

    @pl.when(step == PAIRS)
    def _():
        rows = slice((BLOCKS // 2) * BLOCK, BLOCKS * BLOCK)
        both = [jnp.concatenate([ref[i, rows, :] for i in range(PAIRS)], axis=1) for ref in (probs, grads)]
        store_latents(send_ref, *latent_rows(*both, q_ref, gl_ref))
        turn_keys(early_refs, own_ref[0], early_turned)
        turn_keys(k_refs, own_ref[0], turned)


def keep_kernel(probs_ref, grads_ref, q_ref, gl_ref, keep_ref):
    rows = slice(0, (BLOCKS // 2) * BLOCK)
    both = [jnp.concatenate([ref[i, rows, :] for i in range(PAIRS)], axis=1) for ref in (probs_ref, grads_ref)]
    store_latents(keep_ref, *latent_rows(*both, q_ref, gl_ref))


def diagonal(first, second):
    zero = jnp.zeros_like(first)
    return jnp.concatenate([jnp.concatenate([first, zero], axis=1), jnp.concatenate([zero, second], axis=1)], axis=0)


def weights_kernel(
    own_ref, early_ref, late_ref, probs_ref, grads_ref, query_ref, out_grad_ref, up_key_ref, query_grad_ref, send_ref, keep_ref, up_ref
):
    step = pl.program_id(0)
    share = D_LATENT // CTX

    @pl.when(step == 0)
    def _():
        for position in range(CTX):
            rows = pl.ds(pl.multiple_of((own_ref[0] ^ row_xor(position)) * share, share), share)
            up_ref[position * share : (position + 1) * share, :] = up_key_ref[rows, :]

    half = BLOCKS // 4 * BLOCK
    turned = jnp.concatenate([ref[:, i * half : (i + 1) * half] for i in range(2) for ref in (early_ref, late_ref)], axis=1)
    out_t = dot(turned[:D_LATENT, :], probs_ref[step], NN).astype(BF16)
    abs_t = dot(turned, grads_ref[step], NN) * SCALE
    rope_t = abs_t[D_LATENT:, :]
    abs_t = abs_t[:D_LATENT, :].astype(BF16)
    queries = query_ref[:, pl.ds(pl.multiple_of(step * PAIR_COLS, PAIR_COLS), PAIR_COLS)]
    lanes = pl.ds(pl.multiple_of(step * 2 * NOPE, 2 * NOPE), 2 * NOPE)
    grad_out = out_grad_ref[:, lanes]
    up_key = up_ref[:, lanes]
    width = NOPE + ROPE
    key_part = dot(abs_t, diagonal(queries[:, :NOPE], queries[:, width : width + NOPE]), NN).astype(BF16)
    value_part = dot(out_t, diagonal(grad_out[:, :VDIM], grad_out[:, VDIM:]), NN).astype(BF16)
    for position in range(CTX):
        out = send_ref if position >= CTX // 2 else keep_ref
        rows = slice(position * share, (position + 1) * share)
        out[position % (CTX // 2), 0, :, lanes] = key_part[rows]
        out[position % (CTX // 2), 1, :, lanes] = value_part[rows]
    pieces = []
    for h in range(2):
        cols = slice(h * NOPE, (h + 1) * NOPE)
        pieces.append(dot(abs_t[:, cols], up_key[:, cols], TN))
        pieces.append(rope_t[:, cols].T)
    query_grad_ref[...] = jnp.concatenate(pieces, axis=1).astype(BF16)


def spread_sum(parts):
    total = parts[0].astype(F32)
    for part in parts[1:]:
        total = total + part.astype(F32)
    return total


def in_hbm(*arrays):
    return [pltpu.with_memory_space_constraint(a, pltpu.HBM) for a in arrays]


def in_vmem(*arrays):
    return [pltpu.with_memory_space_constraint(a, pltpu.VMEM) for a in arrays]


def cost(flops, moved):
    return pl.CostEstimate(flops=flops, transcendentals=0, bytes_accessed=moved)


def per_device(queries, latents, rope_key, up_key_weight, up_value_weight, out_grad, group_order):
    tok = queries.shape[0]
    heads = up_key_weight.shape[1] // NOPE
    own = lax.axis_index("ctx").astype(jnp.int32)
    vmem = pl.BlockSpec(memory_space=pltpu.VMEM)
    smem = pl.BlockSpec(memory_space=pltpu.SMEM)
    total = BLOCKS * BLOCK
    half = (CTX // 2) * PACKED
    pair_cols = 2 * (NOPE + ROPE)

    keys = pl.pallas_call(
        pack_kernel,
        out_shape=pltpu.VMEM((PACKED, D_LATENT), BF16),
        in_specs=[vmem] * 2,
        out_specs=vmem,
        compiler_params=pltpu.CompilerParams(vmem_limit_bytes=4 << 20),
        name="pack",
    )(*in_hbm(latents, rope_key.T))
    other = swap_ctx(keys, 2)
    k_chunks = [None] * CTX
    for z, chunk in enumerate((keys, other)):
        near = [chunk]
        for k in (1, 2, 3):
            near.append(swap_ctx(chunk, k << 2))
        for k in range(4):
            k_chunks[4 * z + k] = near[k]
            k_chunks[8 + 4 * z + k] = swap_ctx(near[k], 1)

    query_all, grad_lat, bias = pl.pallas_call(
        prep_kernel,
        grid=(PAIRS,),
        out_shape=(
            jax.ShapeDtypeStruct((PAIRS, 2 * tok, WIDTH), BF16),
            jax.ShapeDtypeStruct((PAIRS, 2 * tok, D_LATENT), BF16),
            jax.ShapeDtypeStruct((total, tok), F32),
        ),
        in_specs=[
            smem,
            smem,
            pl.BlockSpec((tok, pair_cols), lambda i: (0, i)),
            pl.BlockSpec((D_LATENT, 2 * NOPE), lambda i: (0, i)),
            pl.BlockSpec((tok, 2 * VDIM), lambda i: (0, i)),
            pl.BlockSpec((D_LATENT, 2 * VDIM), lambda i: (0, i)),
        ],
        out_specs=(
            pl.BlockSpec((1, 2 * tok, WIDTH), lambda i: (i, 0, 0)),
            pl.BlockSpec((1, 2 * tok, D_LATENT), lambda i: (i, 0, 0)),
            pl.BlockSpec((total // PAIRS, tok), lambda i: (i, 0)),
        ),
        compiler_params=pltpu.CompilerParams(vmem_limit_bytes=8 << 20),
        cost_estimate=cost(300_000_000, 10_000_000),
        name="prep",
    )(own.reshape(1), *in_hbm(group_order, queries, up_key_weight, out_grad, up_value_weight))

    pair_shape = pltpu.VMEM((PAIRS, total, 2 * tok), BF16)
    latent_shape = pltpu.VMEM((half, D_LATENT), BF16)
    early_chunks = [k_chunks[2 * kb + c] for kb in EARLY for c in range(2)]
    late_chunks = [k_chunks[2 * kb + c] for kb in LATE for c in range(2)]
    early = len(EARLY) * BLOCK
    late = len(LATE) * BLOCK
    early_parts = pl.pallas_call(
        early_kernel,
        grid=(PAIRS,),
        out_shape=(
            pltpu.VMEM((PAIRS, early, 2 * tok), BF16),
            pltpu.VMEM((PAIRS, early, 2 * tok), F32),
            pltpu.VMEM((PAIRS, 8, 2 * tok), F32),
        ),
        in_specs=[vmem] * (len(early_chunks) + 3),
        out_specs=(vmem,) * 3,
        scratch_shapes=[pltpu.VMEM((early, WIDTH), BF16)],
        compiler_params=pltpu.CompilerParams(vmem_limit_bytes=16 << 20),
        cost_estimate=cost(3_000_000_000, 10_000_000),
        name="early",
    )(*in_vmem(*early_chunks, query_all, grad_lat, bias))
    probs, grads, latent_send, early_turned, late_turned = pl.pallas_call(
        scores_kernel,
        grid=(PAIRS + 1,),
        out_shape=(pair_shape, pair_shape, latent_shape)
        + (pltpu.VMEM((WIDTH, early), BF16), pltpu.VMEM((WIDTH, late), BF16)),
        in_specs=[smem] + [vmem] * (CTX + 6),
        out_specs=(vmem,) * 5,
        scratch_shapes=[
            pltpu.VMEM((late, WIDTH), BF16),
            pltpu.VMEM((late, 2 * tok), BF16),
            pltpu.VMEM((late, 2 * tok), F32),
        ],
        compiler_params=pltpu.CompilerParams(vmem_limit_bytes=24 << 20),
        cost_estimate=cost(6_000_000_000, 14_000_000),
        name="scores",
    )(own.reshape(1), *in_vmem(*late_chunks, *early_chunks, query_all, grad_lat, bias, *early_parts))

    latent_got = swap_ctx(latent_send, 1)

    latent_keep = pl.pallas_call(
        keep_kernel,
        out_shape=latent_shape,
        in_specs=[vmem] * 4,
        out_specs=vmem,
        compiler_params=pltpu.CompilerParams(vmem_limit_bytes=24 << 20),
        cost_estimate=cost(2_300_000_000, 7_000_000),
        name="keep",
    )(*in_vmem(probs, grads, query_all, grad_lat))

    share = D_LATENT // CTX
    weight_shape = pltpu.VMEM((CTX // 2, 2, share, heads * NOPE), BF16)
    query_grad, weight_send, weight_keep = pl.pallas_call(
        weights_kernel,
        grid=(PAIRS,),
        out_shape=(jax.ShapeDtypeStruct(queries.shape, BF16), weight_shape, weight_shape),
        in_specs=[smem] + [vmem] * 7,
        out_specs=(pl.BlockSpec((tok, pair_cols), lambda i: (0, i)), vmem, vmem),
        scratch_shapes=[pltpu.VMEM((D_LATENT, heads * NOPE), BF16)],
        compiler_params=pltpu.CompilerParams(vmem_limit_bytes=24 << 20),
        cost_estimate=cost(5_000_000_000, 14_000_000),
        name="weights",
    )(own.reshape(1), *in_vmem(early_turned, late_turned, probs, grads, queries, out_grad, up_key_weight))

    pieces = [
        [
            spread_sum([part[(4 * z + k) * PACKED : (4 * z + k + 1) * PACKED] for part in (latent_keep, latent_got)])
            for z in range(2)
        ]
        for k in range(4)
    ]
    pieces = [jnp.concatenate(p, axis=0).astype(BF16) for p in pieces]
    got = [pieces[0]]
    for k in (2, 1, 3):
        got.append(swap_ctx(pieces[k], k << 2))
    other = spread_sum([g[PACKED:] for g in got]).astype(BF16)
    mine = spread_sum([g[:PACKED] for g in got]).astype(BF16)
    first = swap_ctx(other, 2)
    second = swap_both(other, 2, 1)
    third = swap_head(mine, 1)
    mine = spread_sum([mine, first, second, third])
    mine = mine.astype(BF16)
    other = swap_head(mine, 2)
    mine = spread_sum([mine, other]).astype(BF16)
    other = swap_head(mine, 6)
    latent_grad, rope_turned = pl.pallas_call(
        final_kernel,
        out_shape=(jax.ShapeDtypeStruct((tok, D_LATENT), F32), jax.ShapeDtypeStruct((ROPE, tok), F32)),
        in_specs=[vmem] * 2,
        out_specs=(vmem, vmem),
        compiler_params=pltpu.CompilerParams(vmem_limit_bytes=4 << 20),
        name="final",
    )(*in_vmem(mine, other))
    rope_grad = rope_turned.T

    weight_got = swap_ctx(weight_send, 1)
    pieces = [
        spread_sum([weight_keep[2 * k : 2 * k + 2], weight_got[2 * k : 2 * k + 2]]).astype(BF16) for k in range(4)
    ]
    got = [pieces[0]]
    for k in (2, 1, 3):
        got.append(swap_ctx(pieces[k], k << 2))
    other = spread_sum([g[1] for g in got]).astype(BF16)
    other = swap_ctx(other, 2)
    up_key_grad, up_value_grad = (spread_sum([g[0, i] for g in got] + [other[i]]) for i in range(2))
    return query_grad, latent_grad, rope_grad, up_key_grad, up_value_grad


def solution(mesh):
    placed = (
        P("ctx", "head"),
        P("ctx", None),
        P("ctx", None),
        P(None, "head"),
        P(None, "head"),
        P("ctx", "head"),
        P(),
    )
    return jax.shard_map(
        per_device,
        mesh=mesh,
        in_specs=placed,
        out_specs=(
            P("ctx", "head"),
            P("ctx", None),
            P("ctx", None),
            P("ctx", "head"),
            P("ctx", "head"),
        ),
        check_vma=False,
    )
```

```python
import math

import jax
import jax.numpy as jnp
from jax import lax
from jax.experimental import pallas as pl
from jax.experimental.pallas import tpu as pltpu
from jax.sharding import PartitionSpec as P


D_LATENT = 512
ROPE = 64
NOPE = 128
VDIM = 128
WIDTH = D_LATENT + ROPE
GROUP = 64
NEG_FILL = -1e30
SCALE = (NOPE + ROPE) ** -0.5
SCALE_LOG2 = SCALE * math.log2(math.e)

CTX = 16
HEAD = 8
BF16 = jnp.bfloat16
F32 = jnp.float32


def key_xor(position):
    core, zhi, y_bits = position >> 3, (position >> 2) & 1, position & 3
    return (y_bits << 2) | (zhi << 1) | core


def row_xor(position):
    core, y_bits, zhi = position >> 3, (position >> 1) & 3, position & 1
    return (y_bits << 2) | (zhi << 1) | core


def swap_ctx(value, mask):
    return lax.ppermute(value, "ctx", [(i, i ^ mask) for i in range(CTX)])


def swap_head(value, mask):
    return lax.ppermute(value, "head", [(i, i ^ mask) for i in range(HEAD)])


def swap_both(value, ctx_mask, head_mask):
    mask = ctx_mask * HEAD + head_mask
    return lax.ppermute(value, ("ctx", "head"), [(i, i ^ mask) for i in range(CTX * HEAD)])


def dot(a, b, dims):
    return lax.dot_general(a, b, (dims, ((), ())), preferred_element_type=F32)


NT = ((1,), (1,))
NN = ((1,), (0,))
TN = ((0,), (0,))

BLOCK = 256
BLOCKS = 8
PAIRS = 4
CHUNK = 128
ROPE_ROWS = 16
PACKED = CHUNK + ROPE_ROWS
LANES = 128
PAIR_COLS = 2 * (NOPE + ROPE)
TILE = 64
EARLY = (0, 1, 4, 5)
LATE = (2, 3, 6, 7)


def key_ropes(k_ref):
    return rope_rows(k_ref[CHUNK:, :])


def rope_rows(packed):
    return jnp.concatenate([packed[:, g * LANES : (g + 1) * LANES] for g in range(ROPE // ROPE_ROWS)], axis=0)


def pack_kernel(latents_ref, turned_ref, out_ref):
    out_ref[:CHUNK, :] = latents_ref[...]
    for g in range(ROPE // ROPE_ROWS):
        out_ref[CHUNK:, g * LANES : (g + 1) * LANES] = turned_ref[g * ROPE_ROWS : (g + 1) * ROPE_ROWS, :]


def final_kernel(mine_ref, second_ref, first_ref, third_ref, latent_ref, turned_ref):
    total = mine_ref[...].astype(F32) + second_ref[...].astype(F32)
    total = total + (first_ref[...].astype(F32) + third_ref[...].astype(F32))
    latent_ref[...] = total[:CHUNK]
    turned_ref[...] = rope_rows(total[CHUNK:])


def prep_kernel(own_ref, order_ref, query_ref, up_key_ref, out_grad_ref, up_value_ref, q_ref, gl_ref, bias_ref):
    queries = query_ref[...]
    step = pl.program_id(0)
    for h in range(2):
        first = h * (NOPE + ROPE)
        cols = slice(h * NOPE, (h + 1) * NOPE)
        rows = slice(h * CHUNK, (h + 1) * CHUNK)
        q_ref[0, rows, :D_LATENT] = dot(queries[:, first : first + NOPE], up_key_ref[:, cols], NT).astype(BF16)
        q_ref[0, rows, D_LATENT:] = queries[:, first + NOPE : first + NOPE + ROPE]
        gl_ref[0, rows, :] = dot(out_grad_ref[:, cols], up_value_ref[:, cols], NT).astype(BF16)
    own = own_ref[0]
    lane = lax.broadcasted_iota(jnp.int32, (GROUP, CHUNK), 1)
    row = lax.broadcasted_iota(jnp.int32, (GROUP, CHUNK), 0)
    query_pos = jnp.where(lane < GROUP, order_ref[2 * own] * GROUP, order_ref[2 * own + 1] * GROUP - GROUP) + lane
    for c in range(CTX // PAIRS):
        position = step * (CTX // PAIRS) + c
        device = own ^ key_xor(position)
        for g in range(2):
            key_pos = order_ref[2 * device + g] * GROUP + row
            first = c * CHUNK + g * GROUP
            bias_ref[first : first + GROUP, :] = jnp.where(key_pos <= query_pos, 0.0, NEG_FILL).astype(F32)


def latent_rows(probs, grads, q_ref, gl_ref):
    query = q_ref[...].reshape(PAIRS * 2 * CHUNK, WIDTH)
    grad_lat = gl_ref[...].reshape(PAIRS * 2 * CHUNK, D_LATENT)
    both = dot(grads, query, NN) * SCALE
    return both[:, :D_LATENT] + dot(probs, grad_lat, NN), both[:, D_LATENT:]


def store_latents(out_ref, latent, rope):
    for c in range(latent.shape[0] // CHUNK):
        rows = slice(c * CHUNK, (c + 1) * CHUNK)
        top = c * PACKED
        out_ref[top : top + CHUNK, :] = latent[rows].astype(BF16)
        turned = rope[rows].T
        packed = [turned[g * ROPE_ROWS : (g + 1) * ROPE_ROWS] for g in range(ROPE // ROPE_ROWS)]
        out_ref[top + CHUNK : top + PACKED, :] = jnp.concatenate(packed, axis=1).astype(BF16)


def load_keys(k_refs, keys):
    for i, k_ref in enumerate(k_refs):
        rows = slice(i * CHUNK, (i + 1) * CHUNK)
        keys[rows, :D_LATENT] = k_ref[:CHUNK, :]
        keys[rows, D_LATENT:] = key_ropes(k_ref).T


def score_blocks(blocks, step, keys, q_ref, gl_ref, bias_ref, e_ref, g_ref, state):
    q = q_ref[step]
    gl = gl_ref[step]
    tops = []
    for i, kb in enumerate(blocks):
        rows = slice(i * BLOCK, (i + 1) * BLOCK)
        block = keys[rows, :]
        s = dot(block, q, NT)
        g = dot(block[:, :D_LATENT], gl, NT)
        bias = bias_ref[kb * BLOCK : (kb + 1) * BLOCK, :]
        s = s * SCALE_LOG2 + jnp.concatenate([bias, bias], axis=1)
        top = jnp.max(s, axis=0, keepdims=True)
        if state is not None:
            top = jnp.maximum(state[0], top)
        e = jnp.exp2(s - top)
        total = jnp.sum(e, axis=0, keepdims=True)
        weighted = jnp.sum(e * g, axis=0, keepdims=True)
        if state is not None:
            shrink = jnp.exp2(state[0] - top)
            total = state[1] * shrink + total
            weighted = state[2] * shrink + weighted
        state = (top, total, weighted)
        tops.append(top)
        e_ref[rows, :] = e.astype(BF16)
        g_ref[rows, :] = g
    return state, tops


def turn_keys(k_refs, own, turned):
    share = D_LATENT // CTX
    for i, k_ref in enumerate(k_refs):
        cols = slice(i * CHUNK, (i + 1) * CHUNK)
        block = k_ref[:CHUNK, :].T
        for r in range(CTX):
            other = own ^ r
            position = ((other & 1) << 3) | ((other >> 2) << 1) | ((other >> 1) & 1)
            to = pl.ds(pl.multiple_of(position * share, share), share)
            turned[to, cols] = block[r * share : (r + 1) * share, :]
        turned[D_LATENT:, cols] = key_ropes(k_ref)


def early_kernel(*refs):
    count = 2 * len(EARLY)
    k_refs = refs[:count]
    q_ref, gl_ref, bias_ref, e_ref, g_ref, state_ref, keys = refs[count:]
    step = pl.program_id(0)

    @pl.when(step == 0)
    def _():
        load_keys(k_refs, keys)

    state, tops = score_blocks(
        EARLY, step, keys, q_ref, gl_ref, bias_ref, e_ref.at[step], g_ref.at[step], None
    )
    for i, value in enumerate(state + tuple(tops)):
        state_ref[step, i : i + 1, :] = value


def scores_kernel(*refs):
    count = 2 * len(LATE)
    own_ref, k_refs, early_refs = refs[0], refs[1 : count + 1], refs[count + 1 : CTX + 1]
    q_ref, gl_ref, bias_ref, early_e, early_g, early_state = refs[CTX + 1 : CTX + 7]
    probs, grads, send_ref, early_turned, turned, keys, e_ref, g_ref = refs[CTX + 7 :]
    step = pl.program_id(0)

    @pl.when(step == 0)
    def _():
        load_keys(k_refs, keys)

    @pl.when(step < PAIRS)
    def _():
        before = [early_state[step, i : i + 1, :] for i in range(3 + len(EARLY))]
        state, late_tops = score_blocks(
            LATE, step, keys, q_ref, gl_ref, bias_ref, e_ref, g_ref, tuple(before[:3])
        )
        inverse = 1.0 / state[1]
        delta = state[2] * inverse
        parts = [(EARLY, before[3:], early_e.at[step], early_g.at[step]), (LATE, late_tops, e_ref, g_ref)]
        for blocks, tops, e_part, g_part in parts:
            for i, kb in enumerate(blocks):
                factor = jnp.broadcast_to(jnp.exp2(tops[i] - state[0]) * inverse, (TILE, 2 * CHUNK)).astype(BF16)
                for tile in range(BLOCK // TILE):
                    rows = slice(i * BLOCK + tile * TILE, i * BLOCK + (tile + 1) * TILE)
                    to = slice(kb * BLOCK + tile * TILE, kb * BLOCK + (tile + 1) * TILE)
                    p = e_part[rows, :] * factor
                    probs[step, to, :] = p
                    grads[step, to, :] = p * (g_part[rows, :] - delta).astype(BF16)

    @pl.when(step == PAIRS)
    def _():
        rows = slice((BLOCKS // 2) * BLOCK, BLOCKS * BLOCK)
        both = [jnp.concatenate([ref[i, rows, :] for i in range(PAIRS)], axis=1) for ref in (probs, grads)]
        store_latents(send_ref, *latent_rows(*both, q_ref, gl_ref))
        turn_keys(early_refs, own_ref[0], early_turned)
        turn_keys(k_refs, own_ref[0], turned)


def keep_kernel(probs_ref, grads_ref, q_ref, gl_ref, keep_ref):
    rows = slice(0, (BLOCKS // 2) * BLOCK)
    both = [jnp.concatenate([ref[i, rows, :] for i in range(PAIRS)], axis=1) for ref in (probs_ref, grads_ref)]
    store_latents(keep_ref, *latent_rows(*both, q_ref, gl_ref))


def diagonal(first, second):
    zero = jnp.zeros_like(first)
    return jnp.concatenate([jnp.concatenate([first, zero], axis=1), jnp.concatenate([zero, second], axis=1)], axis=0)


def weights_kernel(
    own_ref, early_ref, late_ref, probs_ref, grads_ref, query_ref, out_grad_ref, up_key_ref, query_grad_ref, send_ref, keep_ref, up_ref
):
    step = pl.program_id(0)
    share = D_LATENT // CTX

    @pl.when(step == 0)
    def _():
        for position in range(CTX):
            rows = pl.ds(pl.multiple_of((own_ref[0] ^ row_xor(position)) * share, share), share)
            up_ref[position * share : (position + 1) * share, :] = up_key_ref[rows, :]

    half = BLOCKS // 4 * BLOCK
    turned = jnp.concatenate([ref[:, i * half : (i + 1) * half] for i in range(2) for ref in (early_ref, late_ref)], axis=1)
    out_t = dot(turned[:D_LATENT, :], probs_ref[step], NN).astype(BF16)
    abs_t = dot(turned, grads_ref[step], NN) * SCALE
    rope_t = abs_t[D_LATENT:, :]
    abs_t = abs_t[:D_LATENT, :].astype(BF16)
    queries = query_ref[:, pl.ds(pl.multiple_of(step * PAIR_COLS, PAIR_COLS), PAIR_COLS)]
    lanes = pl.ds(pl.multiple_of(step * 2 * NOPE, 2 * NOPE), 2 * NOPE)
    grad_out = out_grad_ref[:, lanes]
    up_key = up_ref[:, lanes]
    width = NOPE + ROPE
    key_part = dot(abs_t, diagonal(queries[:, :NOPE], queries[:, width : width + NOPE]), NN).astype(BF16)
    value_part = dot(out_t, diagonal(grad_out[:, :VDIM], grad_out[:, VDIM:]), NN).astype(BF16)
    for position in range(CTX):
        out = send_ref if position >= CTX // 2 else keep_ref
        rows = slice(position * share, (position + 1) * share)
        out[position % (CTX // 2), 0, :, lanes] = key_part[rows]
        out[position % (CTX // 2), 1, :, lanes] = value_part[rows]
    pieces = []
    for h in range(2):
        cols = slice(h * NOPE, (h + 1) * NOPE)
        pieces.append(dot(abs_t[:, cols], up_key[:, cols], TN))
        pieces.append(rope_t[:, cols].T)
    query_grad_ref[...] = jnp.concatenate(pieces, axis=1).astype(BF16)


def spread_sum(parts):
    total = parts[0].astype(F32)
    for part in parts[1:]:
        total = total + part.astype(F32)
    return total


def in_hbm(*arrays):
    return [pltpu.with_memory_space_constraint(a, pltpu.HBM) for a in arrays]


def in_vmem(*arrays):
    return [pltpu.with_memory_space_constraint(a, pltpu.VMEM) for a in arrays]


def cost(flops, moved):
    return pl.CostEstimate(flops=flops, transcendentals=0, bytes_accessed=moved)


def per_device(queries, latents, rope_key, up_key_weight, up_value_weight, out_grad, group_order):
    tok = queries.shape[0]
    heads = up_key_weight.shape[1] // NOPE
    own = lax.axis_index("ctx").astype(jnp.int32)
    vmem = pl.BlockSpec(memory_space=pltpu.VMEM)
    smem = pl.BlockSpec(memory_space=pltpu.SMEM)
    total = BLOCKS * BLOCK
    half = (CTX // 2) * PACKED
    pair_cols = 2 * (NOPE + ROPE)

    keys = pl.pallas_call(
        pack_kernel,
        out_shape=pltpu.VMEM((PACKED, D_LATENT), BF16),
        in_specs=[vmem] * 2,
        out_specs=vmem,
        compiler_params=pltpu.CompilerParams(vmem_limit_bytes=4 << 20),
        name="pack",
    )(*in_hbm(latents, rope_key.T))
    other = swap_ctx(keys, 2)
    k_chunks = [None] * CTX
    for z, chunk in enumerate((keys, other)):
        near = [chunk]
        for k in (1, 2, 3):
            near.append(swap_ctx(chunk, k << 2))
        for k in range(4):
            k_chunks[4 * z + k] = near[k]
            k_chunks[8 + 4 * z + k] = swap_ctx(near[k], 1)

    query_all, grad_lat, bias = pl.pallas_call(
        prep_kernel,
        grid=(PAIRS,),
        out_shape=(
            jax.ShapeDtypeStruct((PAIRS, 2 * tok, WIDTH), BF16),
            jax.ShapeDtypeStruct((PAIRS, 2 * tok, D_LATENT), BF16),
            jax.ShapeDtypeStruct((total, tok), F32),
        ),
        in_specs=[
            smem,
            smem,
            pl.BlockSpec((tok, pair_cols), lambda i: (0, i)),
            pl.BlockSpec((D_LATENT, 2 * NOPE), lambda i: (0, i)),
            pl.BlockSpec((tok, 2 * VDIM), lambda i: (0, i)),
            pl.BlockSpec((D_LATENT, 2 * VDIM), lambda i: (0, i)),
        ],
        out_specs=(
            pl.BlockSpec((1, 2 * tok, WIDTH), lambda i: (i, 0, 0)),
            pl.BlockSpec((1, 2 * tok, D_LATENT), lambda i: (i, 0, 0)),
            pl.BlockSpec((total // PAIRS, tok), lambda i: (i, 0)),
        ),
        compiler_params=pltpu.CompilerParams(vmem_limit_bytes=8 << 20),
        cost_estimate=cost(300_000_000, 10_000_000),
        name="prep",
    )(own.reshape(1), *in_hbm(group_order, queries, up_key_weight, out_grad, up_value_weight))

    pair_shape = pltpu.VMEM((PAIRS, total, 2 * tok), BF16)
    latent_shape = pltpu.VMEM((half, D_LATENT), BF16)
    early_chunks = [k_chunks[2 * kb + c] for kb in EARLY for c in range(2)]
    late_chunks = [k_chunks[2 * kb + c] for kb in LATE for c in range(2)]
    early = len(EARLY) * BLOCK
    late = len(LATE) * BLOCK
    early_parts = pl.pallas_call(
        early_kernel,
        grid=(PAIRS,),
        out_shape=(
            pltpu.VMEM((PAIRS, early, 2 * tok), BF16),
            pltpu.VMEM((PAIRS, early, 2 * tok), F32),
            pltpu.VMEM((PAIRS, 8, 2 * tok), F32),
        ),
        in_specs=[vmem] * (len(early_chunks) + 3),
        out_specs=(vmem,) * 3,
        scratch_shapes=[pltpu.VMEM((early, WIDTH), BF16)],
        compiler_params=pltpu.CompilerParams(vmem_limit_bytes=16 << 20),
        cost_estimate=cost(3_000_000_000, 10_000_000),
        name="early",
    )(*in_vmem(*early_chunks, query_all, grad_lat, bias))
    probs, grads, latent_send, early_turned, late_turned = pl.pallas_call(
        scores_kernel,
        grid=(PAIRS + 1,),
        out_shape=(pair_shape, pair_shape, latent_shape)
        + (pltpu.VMEM((WIDTH, early), BF16), pltpu.VMEM((WIDTH, late), BF16)),
        in_specs=[smem] + [vmem] * (CTX + 6),
        out_specs=(vmem,) * 5,
        scratch_shapes=[
            pltpu.VMEM((late, WIDTH), BF16),
            pltpu.VMEM((late, 2 * tok), BF16),
            pltpu.VMEM((late, 2 * tok), F32),
        ],
        compiler_params=pltpu.CompilerParams(vmem_limit_bytes=24 << 20),
        cost_estimate=cost(6_000_000_000, 14_000_000),
        name="scores",
    )(own.reshape(1), *in_vmem(*late_chunks, *early_chunks, query_all, grad_lat, bias, *early_parts))

    latent_got = swap_ctx(latent_send, 1)

    latent_keep = pl.pallas_call(
        keep_kernel,
        out_shape=latent_shape,
        in_specs=[vmem] * 4,
        out_specs=vmem,
        compiler_params=pltpu.CompilerParams(vmem_limit_bytes=24 << 20),
        cost_estimate=cost(2_300_000_000, 7_000_000),
        name="keep",
    )(*in_vmem(probs, grads, query_all, grad_lat))

    share = D_LATENT // CTX
    weight_shape = pltpu.VMEM((CTX // 2, 2, share, heads * NOPE), BF16)
    query_grad, weight_send, weight_keep = pl.pallas_call(
        weights_kernel,
        grid=(PAIRS,),
        out_shape=(jax.ShapeDtypeStruct(queries.shape, BF16), weight_shape, weight_shape),
        in_specs=[smem] + [vmem] * 7,
        out_specs=(pl.BlockSpec((tok, pair_cols), lambda i: (0, i)), vmem, vmem),
        scratch_shapes=[pltpu.VMEM((D_LATENT, heads * NOPE), BF16)],
        compiler_params=pltpu.CompilerParams(vmem_limit_bytes=24 << 20),
        cost_estimate=cost(5_000_000_000, 14_000_000),
        name="weights",
    )(own.reshape(1), *in_vmem(early_turned, late_turned, probs, grads, queries, out_grad, up_key_weight))

    pieces = [
        [
            spread_sum([part[(4 * z + k) * PACKED : (4 * z + k + 1) * PACKED] for part in (latent_keep, latent_got)])
            for z in range(2)
        ]
        for k in range(4)
    ]
    pieces = [jnp.concatenate(p, axis=0).astype(BF16) for p in pieces]
    got = [pieces[0]]
    for k in (2, 1, 3):
        got.append(swap_ctx(pieces[k], k << 2))
    other = spread_sum([g[PACKED:] for g in got]).astype(BF16)
    mine = spread_sum([g[:PACKED] for g in got]).astype(BF16)
    first = swap_ctx(other, 2)
    second = swap_both(other, 2, 1)
    third = swap_head(mine, 1)
    mine = (spread_sum([mine, third]) + spread_sum([first, second])).astype(BF16)
    others = []
    for mask in (4, 2, 6):
        others.append(swap_head(mine, mask))
    latent_grad, rope_turned = pl.pallas_call(
        final_kernel,
        out_shape=(jax.ShapeDtypeStruct((tok, D_LATENT), F32), jax.ShapeDtypeStruct((ROPE, tok), F32)),
        in_specs=[vmem] * 4,
        out_specs=(vmem, vmem),
        compiler_params=pltpu.CompilerParams(vmem_limit_bytes=4 << 20),
        name="final",
    )(*in_vmem(mine, *others))
    rope_grad = rope_turned.T

    weight_got = swap_ctx(weight_send, 1)
    pieces = [
        spread_sum([weight_keep[2 * k : 2 * k + 2], weight_got[2 * k : 2 * k + 2]]).astype(BF16) for k in range(4)
    ]
    got = [pieces[0]]
    for k in (2, 1, 3):
        got.append(swap_ctx(pieces[k], k << 2))
    other = spread_sum([g[1] for g in got]).astype(BF16)
    other = swap_ctx(other, 2)
    up_key_grad, up_value_grad = (spread_sum([g[0, i] for g in got] + [other[i]]) for i in range(2))
    return query_grad, latent_grad, rope_grad, up_key_grad, up_value_grad


def solution(mesh):
    placed = (
        P("ctx", "head"),
        P("ctx", None),
        P("ctx", None),
        P(None, "head"),
        P(None, "head"),
        P("ctx", "head"),
        P(),
    )
    return jax.shard_map(
        per_device,
        mesh=mesh,
        in_specs=placed,
        out_specs=(
            P("ctx", "head"),
            P("ctx", None),
            P("ctx", None),
            P("ctx", "head"),
            P("ctx", "head"),
        ),
        check_vma=False,
    )
```
